32 devices in a mesh: row: 4 (over z), col: 2 (over x), rep: 4 (over y, core).
Axes of the slice: x: 2, y: 2, z: 4, core: 2. Of those that a mesh axis runs over, the one named last changes fastest.
Arguments:
- density: bfloat16 [1536, 1536], P('row', 'col'), as said below
- keep_square: int32 [12, 12], P('row', 'col'), may hold values 0 or 1
- keep_cube: int32 [12, 12], P('row', 'col'), may hold values 0 or 1
Outputs:
- purified: float32 [1536, 1536], P(('row', 'rep'), 'col')
The draws below stay inside these ranges and needn't reach their ends.
Inputs may be any that keep to these rules, and one draw needn't show every extreme that they name: density is symmetric; its 128 x 128 diagonal blocks are always occupied, any other block may be zero or occupied at any distance from the diagonal.
All inputs are finite; a program needn't handle non-finite values. No bound on the sum of `keep_square` or of `keep_cube` on one device may be relied on, other than what follows from the above.
Results may differ from the reference program's by a relative error of at most 0.002.
Values may be sent and summed in bfloat16 or wider, within the bound.
A program may use at most 64 MiB of HBM per device.

```python
import jax
import jax.numpy as jnp

BLK = 128
MAT = 1536
NBLK = 12


def draw_density(key, part):
    block_count = MAT // BLK
    key_bits, key_values = jax.random.split(jax.random.fold_in(key, 17), 2)
    raw_bits = jax.random.randint(key_bits, (block_count, block_count), 0, 4)
    upper = jnp.triu((raw_bits == 0).astype(jnp.int32), 1)
    pattern = upper + upper.T + jnp.eye(block_count, dtype=jnp.int32) > 0
    blocks = jnp.broadcast_to(pattern.astype(jnp.float32)[:, None, :, None], (block_count, BLK, block_count, BLK)).reshape(MAT, MAT)
    values = jax.random.normal(key_values, (MAT, MAT), jnp.float32)
    values = (values + values.T) * 0.7071
    return (values * blocks * ((block_count // 4 + 1) * BLK * 1.0) ** (-0.25)).astype(jnp.bfloat16)


def plant(result, key, low, top_value):
    index_at = [jax.random.randint(jax.random.fold_in(key, axis), (), 0, length) for axis, length in enumerate(result.shape)]
    widest = result.shape.index(max(result.shape))
    next_to = index_at[:widest] + [(index_at[widest] + 1) % result.shape[widest]] + index_at[widest + 1:]
    return result.at[tuple(index_at)].set(low).at[tuple(next_to)].set(top_value)


def setup_inputs(seed: int = 0) -> dict:
    keys = jax.random.split(jax.random.key(seed), 4)
    density = draw_density(jax.random.fold_in(keys[3], 71), 0)
    keep_square = plant((jax.random.randint(keys[1], (NBLK, NBLK), 0, 4) < 3).astype(jnp.int32), jax.random.fold_in(keys[1], 1), 0, 1)
    keep_cube = plant((jax.random.randint(keys[2], (NBLK, NBLK), 0, 4) < 3).astype(jnp.int32), jax.random.fold_in(keys[2], 1), 0, 1)
    return dict(density=density, keep_square=keep_square, keep_cube=keep_cube)


def widen(mask):
    count = mask.shape[0]
    blocks = jnp.broadcast_to(mask.astype(jnp.float32)[:, None, :, None], (count, BLK, count, BLK))
    return blocks.reshape(count * BLK, count * BLK)


def reference(density, keep_square, keep_cube):
    square = jnp.dot(density, density, preferred_element_type=jnp.float32) * widen(keep_square)
    square_low = square.astype(jnp.bfloat16)
    cube = jnp.dot(square_low, density, preferred_element_type=jnp.float32) * widen(keep_cube)
    return 3.0 * square - 2.0 * cube
```

```python
import functools

import jax
import jax.numpy as jnp
from jax import lax
from jax.experimental import pallas as pl
from jax.experimental.pallas import tpu as pltpu
from jax.sharding import PartitionSpec as P

MESH = pl.DeviceIdType.MESH

def flip(index, bit):
    return index + bit - 2 * bit * (index // bit % 2)


def panel_kernel(rows, cols, reps, block, chunks, density, keep_square, keep_cube, out,
           panel, left, low, total, z_send, z_recv, r_send, r_recv, a_send, a_recv,
           l_send, l_recv, local_sem):
    tile_rows, tile_cols = density.shape
    own = tile_rows // reps
    piece = own // chunks
    ratio = tile_cols // tile_rows
    z, c, p = lax.axis_index("row"), lax.axis_index("col"), lax.axis_index("rep")
    bits = []
    bit = reps // 2
    while bit:
        bits.append(bit)
        bit //= 2
    others = [lax.rem(c + step, cols) for step in range(1, cols)]

    barrier = pltpu.get_barrier_semaphore()
    for step, ok in ((1, z < rows - 1), (-1, z > 0)):
        @pl.when(ok)
        def _():
            pl.semaphore_signal(barrier, inc=1, device_id={"row": z + step}, device_id_type=MESH)
    for bit in bits:
        pl.semaphore_signal(barrier, inc=1, device_id={"rep": flip(p, bit)}, device_id_type=MESH)
    for other in others:
        pl.semaphore_signal(barrier, inc=1, device_id={"col": other}, device_id_type=MESH)
    keep_tile = pltpu.make_async_copy(
        density, panel.at[pl.ds(pl.multiple_of(z * tile_rows, tile_rows), tile_rows)], local_sem.at[0])
    keep_tile.start()
    keep_left = [
        pltpu.make_async_copy(
            density.at[pl.ds(pl.multiple_of(p * own, own), own), pl.ds(part * tile_rows, tile_rows)],
            left.at[c * ratio + part], local_sem.at[1 + part])
        for part in range(ratio)
    ]
    for copy in keep_left:
        copy.start()
    below, above = (z + rows - 1) // rows, (2 * rows - 2 - z) // rows
    pl.semaphore_wait(barrier, len(bits) + len(others) + below + above)

    def slot(t, member, q):
        return panel.at[pl.ds(pl.multiple_of(t * tile_rows + member * own + q * piece, piece), piece)]

    def packed(t, place):
        return t - (t - place - 1 + rows) // rows

    def z_copy(t, q, step, first=False, sending=True):
        at = z if sending else z - step
        source = slot(t, p, q)
        if first:
            source = density.at[pl.ds(pl.multiple_of(p * own + q * piece, piece), piece)]
        return pltpu.make_async_remote_copy(
            source, slot(t, p, q), z_send.at[t + (1 - step) // 2, q],
            z_recv.at[packed(t, at + step), q],
            device_id={"row": z + step}, device_id_type=MESH)

    def r_copies(t, q, stage):
        members = [p]
        for bit in bits[:stage]:
            members = members + [flip(member, bit) for member in members]
        peer = flip(p, bits[stage])
        base = 2 ** stage - 1
        return [
            pltpu.make_async_remote_copy(
                slot(t, member, q), slot(t, member, q), r_send.at[base + i, packed(t, z), q],
                r_recv.at[base + i, packed(t, z), q], device_id={"rep": peer}, device_id_type=MESH)
            for i, member in enumerate(members)
        ]

    def r_waits(t, q, stage):
        peer = flip(p, bits[stage])
        members = [peer]
        for bit in bits[:stage]:
            members = members + [flip(member, bit) for member in members]
        base = 2 ** stage - 1
        for i, member in enumerate(members):
            pltpu.make_async_remote_copy(
                slot(t, member, q), slot(t, member, q), r_send.at[base + i, packed(t, z), q],
                r_recv.at[base + i, packed(t, z), q], device_id={"rep": peer}, device_id_type=MESH).wait_recv()

    def a_copy(owner, peer, part):
        return pltpu.make_async_remote_copy(
            density.at[pl.ds(pl.multiple_of(p * own, own), own), pl.ds(part * tile_rows, tile_rows)],
            left.at[owner * ratio + part], a_send.at[peer, part], a_recv.at[owner, part],
            device_id={"col": peer}, device_id_type=MESH)

    def l_copy(owner, peer, part):
        return pltpu.make_async_remote_copy(
            low.at[owner * ratio + part], low.at[owner * ratio + part],
            l_send.at[peer, part], l_recv.at[owner, part],
            device_id={"col": peer}, device_id_type=MESH)

    ways = ((1, z < rows - 1), (-1, z > 0))
    for q in range(chunks):
        for step, ok in ways:
            @pl.when(ok)
            def _():
                z_copy(z, q, step, True).start()
    for other in others:
        for part in range(ratio):
            a_copy(c, other, part).start()

    def arrivals(distance):
        return ((1, z - distance, z - distance >= 0, z < rows - 1),
                (-1, z + distance, z + distance < rows, z > 0))

    def take(distance):
        for q in range(chunks):
            for step, t, ok, onward in arrivals(distance):
                @pl.when(ok)
                def _():
                    z_copy(t, q, step, sending=False).wait_recv()

                    @pl.when(onward)
                    def _():
                        z_copy(t, q, step).start()
                    for copy in r_copies(t, q, 0):
                        copy.start()

    def spread(distance, stage):
        for q in range(chunks):
            for step, t, ok, onward in arrivals(distance):
                @pl.when(ok)
                def _():
                    r_waits(t, q, stage - 1)
                    for copy in r_copies(t, q, stage):
                        copy.start()

    def product(factor, t):
        return jnp.dot(factor[t], panel[pl.ds(pl.multiple_of(t * tile_rows, tile_rows), tile_rows), :],
                       preferred_element_type=jnp.float32)

    def use(distance):
        for step, t, ok, onward in arrivals(distance):
            @pl.when(ok)
            def _():
                for q in range(chunks):
                    r_waits(t, q, len(bits) - 1)
                total[...] += product(left, t)

    keep_tile.wait()
    for copy in keep_left:
        copy.wait()
    started = False
    for distance in range(1, rows + len(bits)):
        if distance < rows:
            take(distance)
        for stage in range(1, len(bits)):
            if 1 <= distance - stage < rows:
                spread(distance - stage, stage)
        if not started:
            for other in others:
                for part in range(ratio):
                    a_copy(other, other, part).wait_recv()
            total[...] = product(left, z)
            started = True
        if 1 <= distance - len(bits) < rows:
            use(distance - len(bits))

    row_block = (p * own + lax.broadcasted_iota(jnp.int32, (own, block), 0)) // block

    def widen(keep, column):
        wide = jnp.zeros((own, block), jnp.float32)
        for i in range(tile_rows // block):
            wide = jnp.where(row_block == i, keep[i, column].astype(jnp.float32), wide)
        return wide

    per_part = tile_rows // block
    for column in range(tile_cols // block):
        span = pl.ds(column * block, block)
        square = total[:, span] * widen(keep_square, column)
        total[:, span] = square
        low[c * ratio + column // per_part, :, pl.ds(column % per_part * block, block)] = square.astype(jnp.bfloat16)
    for other in others:
        for part in range(ratio):
            l_copy(c, other, part).start()
    cube = product(low, c * ratio)
    for part in range(1, ratio):
        cube = cube + product(low, c * ratio + part)
    out[...] = cube
    for other in others:
        for part in range(ratio):
            l_copy(other, other, part).wait_recv()
            out[...] += product(low, other * ratio + part)
    for column in range(tile_cols // block):
        span = pl.ds(column * block, block)
        out[:, span] = 3.0 * total[:, span] - 2.0 * (out[:, span] * widen(keep_cube, column))

    for q in range(chunks):
        for step, ok in ways:
            @pl.when(ok)
            def _():
                z_copy(z, q, step, True).wait_send()
        for distance in range(1, rows):
            for step, t, ok, onward in arrivals(distance):
                @pl.when(ok)
                def _():
                    @pl.when(onward)
                    def _():
                        z_copy(t, q, step).wait_send()
                    for stage in range(len(bits)):
                        for copy in r_copies(t, q, stage):
                            copy.wait_send()
    for other in others:
        for part in range(ratio):
            a_copy(c, other, part).wait_send()
            l_copy(c, other, part).wait_send()


def by_panel(rows, cols, reps, mat, density, keep_square, keep_cube):
    tile_rows, tile_cols = density.shape
    block = tile_rows // keep_square.shape[0]
    own = tile_rows // reps
    ratio = tile_cols // tile_rows
    chunks = 3 if own % 48 == 0 else 1
    dma = pltpu.SemaphoreType.DMA
    return pl.pallas_call(
        functools.partial(panel_kernel, rows, cols, reps, block, chunks),
        out_shape=pltpu.VMEM((own, tile_cols), jnp.float32),
        in_specs=[
            pl.BlockSpec(memory_space=pl.ANY),
            pl.BlockSpec(memory_space=pltpu.SMEM),
            pl.BlockSpec(memory_space=pltpu.SMEM),
        ],
        out_specs=pl.BlockSpec(memory_space=pltpu.VMEM),
        scratch_shapes=[
            pltpu.VMEM((mat, tile_cols), jnp.bfloat16),
            pltpu.VMEM((rows, own, tile_rows), jnp.bfloat16),
            pltpu.VMEM((rows, own, tile_rows), jnp.bfloat16),
            pltpu.VMEM((own, tile_cols), jnp.float32),
            dma((rows + 1, chunks)),
            dma((rows - 1, chunks)),
            dma((reps - 1, rows - 1, chunks)),
            dma((reps - 1, rows - 1, chunks)),
            dma((cols, ratio)),
            dma((cols, ratio)),
            dma((cols, ratio)),
            dma((cols, ratio)),
            dma((1 + ratio,)),
        ],
        compiler_params=pltpu.CompilerParams(collective_id=0, has_side_effects=True),
    )(density, keep_square, keep_cube)


STREAMS = ("x_keep", "x_own", "y_own", "z_diag", "x_diag", "z_off", "y_off",
           "c_part", "x_part", "y_part", "v_part", "t_far", "t_diag", "t_off", "t_part")


def whole_kernel(reps, block, density, keep_square, keep_cube, out,
                 tiles, cross, corner, keeps, square, low, keep_wide, local_sem, ready, *sems):
    streams = {name: sems[2 * i:2 * i + 2] for i, name in enumerate(STREAMS)}
    tile, wide = density.shape
    own = tile // reps
    strips = tile // block
    sub = block // reps
    every = range(strips)
    z, c, p = lax.axis_index("row"), lax.axis_index("col"), lax.axis_index("rep")
    half, here = z // 2, z % 2
    there, other, far = 1 - here, 1 - half, 1 - c
    across = p + reps // 2 - reps * (p // (reps // 2))
    twin = p + 1 - 2 * (p % 2)
    is_diag, is_inner = c == half, here != half
    to_far, to_mate = {"col": far}, {"row": z + 1 - 2 * here}
    to_across, to_twin, to_corner = {"rep": across}, {"rep": twin}, {"col": far, "rep": across}
    quarters = (p, across)
    twins = (twin, across + 1 - 2 * (across % 2))
    distant = (3 * other, other + 1)
    near, end = 1 - other, other
    from_far, from_diag = (0, 2), (1, 3, 4, 5)

    def remote(source, target, name, index, device, arrival=None):
        send, recv = streams[name]
        return pltpu.make_async_remote_copy(
            source, target, send.at[index], recv.at[index if arrival is None else arrival],
            device_id=device, device_id_type=MESH)

    def rows(q, s):
        return pl.ds(pl.multiple_of(s * block + q * sub, sub), sub)

    def columns(start, size):
        return pl.ds(pl.multiple_of(start, block), size)

    def level_at(level):
        return columns(level * tile, tile)

    def relay(ref, name, index, device):
        return remote(ref, ref, name, index, device)

    def own_out(name, q, s, device):
        return remote(density.at[rows(q, s)], tiles.at[c, here, rows(q, s)], name, s, device)

    def tile_at(column, level, q, s):
        return tiles.at[column, level, rows(q, s)]

    def diag_at(level, q, s):
        return tiles.at[half, level, rows(q, s), columns(level * tile + s * block, tile - s * block)]

    def part_at(i, q, of=other, source=False):
        if i < strips:
            band = of * i + (1 - of) * (strips - 1 - i)
            ref = density if source else cross
            return ref.at[rows(q, band), columns(of * i * block, wide - i * block)]
        i = i - strips
        if source:
            return density.at[rows(q, i), columns(here * tile + i * block, tile - i * block)]
        return corner.at[rows(q, i), columns(i * block, tile - i * block)]

    def part_out(i, d, column):
        source = part_at(i, p, half, True)
        target = part_at(i, p, half)
        return remote(source, target, "c_part", 2 * i + d, {"row": distant[d], "col": column}, i)

    def part_in(i):
        return relay(part_at(i, p), "c_part", i, to_mate)

    def far_parts(name, i, q, device):
        return relay(part_at(i, q), name, i, device)

    def twin_part(j, i, incoming=False):
        return relay(part_at(i, (twins if incoming else quarters)[j]), "t_part", j * 2 * strips + i, to_twin)

    def twin_tile(name, column, level, j, s, incoming=False):
        return relay(tile_at(column, level, (twins if incoming else quarters)[j], s), name, j * strips + s, to_twin)

    def twin_diag(j, s, incoming=False):
        return relay(diag_at(there, (twins if incoming else quarters)[j], s), "t_diag", j * strips + s, to_twin)

    def keep_copy(at):
        return remote(keep_square, keeps.at[at], "x_keep", 0, to_far)

    def spread(i):
        part_in(i).wait_recv()
        far_parts("x_part", i, p, to_far).start()
        far_parts("y_part", i, p, to_across).start()
        far_parts("v_part", i, p, to_corner).start()
        twin_part(0, i).start()

    def gather(mine, theirs):
        for i in theirs:
            far_parts("x_part", i, p, to_far).wait_recv()
            twin_part(0, i).start()
        for i in mine:
            far_parts("y_part", i, across, to_across).wait_recv()
            twin_part(1, i).start()
        for i in theirs:
            far_parts("v_part", i, across, to_corner).wait_recv()
            twin_part(1, i).start()

    barrier = pltpu.get_barrier_semaphore()
    beside = (to_far, to_mate, to_across, to_twin, to_corner)
    for device in beside:
        pl.semaphore_signal(barrier, inc=1, device_id=device, device_id_type=MESH)
    is_low = half == 0

    @pl.when(is_low)
    def _():
        for at in distant:
            pl.semaphore_signal(barrier, inc=1, device_id={"row": at, "col": other}, device_id_type=MESH)

    @pl.when(is_low & is_diag)
    def _():
        for at in distant:
            for column in (c, far):
                pl.semaphore_signal(barrier, inc=1, device_id={"row": at, "col": column}, device_id_type=MESH)

    tile_copy = pltpu.make_async_copy(density, tiles.at[c, here], local_sem.at[0])
    tile_copy.start()
    keep_local = pltpu.make_async_copy(keep_square, keeps.at[c], local_sem.at[1])
    keep_local.start()

    row_block = (p * own + lax.broadcasted_iota(jnp.int32, (own, block), 0)) // block

    def widen(at, keep, scale):
        for column in range(wide // block):
            value = jnp.zeros((own, block), jnp.float32)
            for i in range(tile // block):
                value = jnp.where(row_block == i, keep(i, column).astype(jnp.float32) * scale, value)
            keep_wide[at, :, pl.ds(column * block, block)] = value

    def widen_own():
        widen(2, lambda i, j: keep_cube[i, j], -2.0)
        keep_local.wait()
        widen(c, lambda i, j: keeps[c, i, j], 1.0)

    def parts_out(done=False):
        for d in range(2):
            @pl.when(is_inner)
            def _():
                for i in (1, 0, 2):
                    copy = part_out(i, d, far if i in from_diag else c)
                    copy.wait_send() if done else copy.start()

            @pl.when(jnp.logical_not(is_inner))
            def _():
                for i in range(strips, 2 * strips):
                    copy = part_out(i, d, far)
                    copy.wait_send() if done else copy.start()

    @pl.when(is_low)
    def _():
        pl.semaphore_wait(barrier, len(beside))

    @pl.when(jnp.logical_not(is_low))
    def _():
        @pl.when(is_diag)
        def _():
            pl.semaphore_wait(barrier, len(beside) + 6)
            parts_out()

        @pl.when(jnp.logical_not(is_diag))
        def _():
            pl.semaphore_wait(barrier, len(beside) + 2)
        for at in distant:
            pl.semaphore_signal(ready, inc=1, device_id={"row": at, "col": other}, device_id_type=MESH)

    keep_copy(c).start()
    for s in every:
        own_out("x_own", p, s, to_far).start()

    @pl.when(is_diag)
    def _():
        for j in range(2):
            for s in every:
                remote(density.at[rows(quarters[j], s), columns(here * tile + s * block, tile - s * block)],
                       diag_at(here, quarters[j], s), "z_diag", j * strips + s, to_mate).start()

        @pl.when(is_low)
        def _():
            pl.semaphore_wait(ready, 4)
            parts_out()
        widen_own()
        for s in every:
            relay(tile_at(other, here, p, s), "x_own", s, to_far).wait_recv()
            relay(tile_at(other, here, p, s), "y_own", s, to_across).start()
            relay(tile_at(other, here, p, s), "z_off", s, to_mate).start()
            twin_tile("t_far", other, here, 0, s).start()
        for j in range(2):
            for s in every:
                relay(diag_at(there, quarters[j], s), "z_diag", j * strips + s, to_mate).wait_recv()
                relay(diag_at(there, quarters[j], s), "x_diag", j * strips + s, to_far).start()
                twin_diag(j, s).start()
        for s in every:
            relay(tile_at(other, here, across, s), "y_own", s, to_across).wait_recv()
            relay(tile_at(other, here, across, s), "z_off", strips + s, to_mate).start()
            twin_tile("t_far", other, here, 1, s).start()
        for i in from_diag:
            spread(i)
        for s in every:
            relay(tile_at(other, there, p, s), "z_off", s, to_mate).wait_recv()
            twin_tile("t_off", other, there, 0, s).start()

    @pl.when(jnp.logical_not(is_diag))
    def _():
        for s in every:
            own_out("z_off", p, s, to_mate).start()
        widen_own()
        for s in every:
            relay(tile_at(other, there, p, s), "z_off", s, to_mate).wait_recv()
            relay(tile_at(other, there, p, s), "y_off", s, to_across).start()
            twin_tile("t_off", other, there, 0, s).start()
        for s in every:
            relay(tile_at(half, here, p, s), "x_own", s, to_far).wait_recv()
            relay(tile_at(half, here, p, s), "y_own", s, to_across).start()
            twin_tile("t_far", half, here, 0, s).start()
        for i in from_far:
            spread(i)
        for s in every:
            relay(tile_at(half, here, across, s), "y_own", s, to_across).wait_recv()
            twin_tile("t_far", half, here, 1, s).start()
        for j in range(2):
            for s in every:
                relay(diag_at(there, quarters[j], s), "x_diag", j * strips + s, to_far).wait_recv()
                twin_diag(j, s).start()

    tile_copy.wait()
    keep_copy(far).wait_recv()
    widen(far, lambda i, j: keeps[far, i, j], 1.0)

    def dot(a, b, contract=0):
        return lax.dot_general(a, b, (((1,), (contract,)), ((), ())), preferred_element_type=jnp.float32)

    def complete(ref, lead, level, source_first):
        for a in every:
            for b in range(a + 1, strips):
                r, t = (a, b) if source_first is None else (b + source_first * (a - b), a + source_first * (b - a))
                block_at = lambda i, j: lead + (columns(i * block, block), columns(level * tile + j * block, block))
                ref[block_at(t, r)] = ref[block_at(r, t)].T

    def by_diag(left_here, left_there):
        a = tiles[half, here, :, level_at(here)]
        b = tiles[half, here, :, level_at(there)]
        d = tiles[half, there, :, level_at(there)]
        return dot(left_here, a) + dot(left_there, b, 1), dot(left_here, b) + dot(left_there, d)

    def by_cross(left_near, left_end):
        a = cross[:, level_at(near)]
        b = cross[:, level_at(end)]
        return dot(left_near, a) + dot(left_end, b, 1), dot(left_near, b) + dot(left_end, corner[...])

    my_rows = pl.ds(pl.multiple_of(p * own, own), own)

    for j in range(2):
        for s in every:
            twin_diag(j, s, True).wait_recv()
            twin_tile("t_far", far, here, j, s, True).wait_recv()
    complete(tiles, (half, there), there, None)
    lh = [tiles[half, here, my_rows, level_at(level)] for level in (here, there)]
    lo = tiles[other, here, my_rows, :]
    h_here, h_there = by_diag(*lh)
    square[half, :, level_at(here)] = h_here + dot(lo, tiles[other, here], 1)
    square[half, :, level_at(there)] = h_there
    square[other] = dot(lh[0], tiles[other, here])

    @pl.when(is_diag)
    def _():
        gather(from_diag, from_far)
        for s in every:
            relay(tile_at(other, there, across, s), "z_off", strips + s, to_mate).wait_recv()
            twin_tile("t_off", other, there, 1, s).start()

    @pl.when(jnp.logical_not(is_diag))
    def _():
        for s in every:
            relay(tile_at(other, there, across, s), "y_off", s, to_across).wait_recv()
            twin_tile("t_off", other, there, 1, s).start()
        gather(from_far, from_diag)

    for j in range(2):
        for s in every:
            twin_tile("t_off", other, there, j, s, True).wait_recv()

    def mask(at):
        value = square[at] * keep_wide[at]
        square[at] = value
        low[at] = value.astype(jnp.bfloat16)

    square[half, :, level_at(there)] += dot(lo, tiles[other, there], 1)
    mask(half)
    square[other] += dot(lh[1], tiles[other, there])

    @pl.when(is_diag)
    def _():
        h_here, h_there = by_diag(low[half, :, level_at(here)], low[half, :, level_at(there)])
        out[:, level_at(here)] = h_here
        out[:, level_at(there)] = h_there

    @pl.when(jnp.logical_not(is_diag))
    def _():
        out[...] = (dot(low[half, :, level_at(here)], tiles[other, here])
                    + dot(low[half, :, level_at(there)], tiles[other, there]))

    for j in range(2):
        for i in range(2 * strips):
            twin_part(j, i, True).wait_recv()
    complete(cross, (), near, other)
    complete(corner, (), 0, None)
    o_near, o_end = by_cross(*(tiles[other, here, my_rows, level_at(level)] for level in (near, end)))
    square[other, :, level_at(near)] += o_near
    square[other, :, level_at(end)] += o_end
    mask(other)

    @pl.when(is_diag)
    def _():
        for level in (here, there):
            span = level_at(level)
            cube = out[:, span] + dot(low[other], tiles[other, level], 1)
            out[:, span] = 3.0 * square[c, :, span] + cube * keep_wide[2, :, span]

    @pl.when(jnp.logical_not(is_diag))
    def _():
        cubes = by_cross(low[other, :, level_at(near)], low[other, :, level_at(end)])
        for level, part in zip((near, end), cubes):
            span = level_at(level)
            cube = out[:, span] + part
            out[:, span] = 3.0 * square[c, :, span] + cube * keep_wide[2, :, span]

    keep_copy(c).wait_send()
    for s in every:
        own_out("x_own", p, s, to_far).wait_send()
        relay(tile_at(far, here, p, s), "y_own", s, to_across).wait_send()
        for j in range(2):
            twin_tile("t_far", far, here, j, s).wait_send()
            twin_tile("t_off", other, there, j, s).wait_send()
            twin_diag(j, s).wait_send()
    for j in range(2):
        for i in range(2 * strips):
            twin_part(j, i).wait_send()

    def spread_sent(mine):
        for i in mine:
            far_parts("x_part", i, p, to_far).wait_send()
            far_parts("y_part", i, p, to_across).wait_send()
            far_parts("v_part", i, p, to_corner).wait_send()

    @pl.when(is_diag)
    def _():
        spread_sent(from_diag)
        parts_out(done=True)
        for j in range(2):
            for s in every:
                relay(diag_at(here, quarters[j], s), "z_diag", j * strips + s, to_mate).wait_send()
                relay(diag_at(there, quarters[j], s), "x_diag", j * strips + s, to_far).wait_send()
                relay(tile_at(other, here, quarters[j], s), "z_off", j * strips + s, to_mate).wait_send()

    @pl.when(jnp.logical_not(is_diag))
    def _():
        spread_sent(from_far)
        for s in every:
            own_out("z_off", p, s, to_mate).wait_send()
            relay(tile_at(other, there, p, s), "y_off", s, to_across).wait_send()


def by_whole(reps, density, keep_square, keep_cube):
    tile, wide = density.shape
    block = tile // keep_square.shape[0]
    own = tile // reps
    strips = tile // block
    dma = pltpu.SemaphoreType.DMA
    low = jnp.bfloat16
    return pl.pallas_call(
        functools.partial(whole_kernel, reps, block),
        out_shape=pltpu.VMEM((own, wide), jnp.float32),
        in_specs=[
            pl.BlockSpec(memory_space=pl.ANY),
            pl.BlockSpec(memory_space=pl.ANY),
            pl.BlockSpec(memory_space=pltpu.SMEM),
        ],
        out_specs=pl.BlockSpec(memory_space=pltpu.VMEM),
        scratch_shapes=[
            pltpu.VMEM((2, 2, tile, wide), low),
            pltpu.VMEM((tile, wide), low),
            pltpu.VMEM((tile, tile), low),
            pltpu.SMEM((2,) + keep_square.shape, jnp.int32),
            pltpu.VMEM((2, own, wide), jnp.float32),
            pltpu.VMEM((2, own, wide), low),
            pltpu.VMEM((3, own, wide), jnp.float32),
            dma((2,)),
            pltpu.SemaphoreType.REGULAR,
        ] + [dma((4 * strips,))] * (2 * len(STREAMS)),
        compiler_params=pltpu.CompilerParams(collective_id=0, has_side_effects=True),
    )(density, keep_square, keep_cube)


def solution(mesh):
    rows, cols, reps = (mesh.shape[axis] for axis in ("row", "col", "rep"))

    def body(density, keep_square, keep_cube):
        tile, wide = density.shape
        if cols == 2 and rows == 2 * cols and reps == 4 and tile * rows == wide * cols:
            return by_whole(reps, density, keep_square, keep_cube)
        return by_panel(rows, cols, reps, tile * rows, density, keep_square, keep_cube)

    return jax.shard_map(
        body,
        mesh=mesh,
        in_specs=(P("row", "col"), P("row", "col"), P("row", "col")),
        out_specs=P(("row", "rep"), "col"),
        check_vma=False,
    )
```

```python
import functools

import jax
import jax.numpy as jnp
from jax import lax
from jax.experimental import pallas as pl
from jax.experimental.pallas import tpu as pltpu
from jax.sharding import PartitionSpec as P

MESH = pl.DeviceIdType.MESH

def flip(index, bit):
    return index + bit - 2 * bit * (index // bit % 2)


def panel_kernel(rows, cols, reps, block, chunks, density, keep_square, keep_cube, out,
           panel, left, low, total, z_send, z_recv, r_send, r_recv, a_send, a_recv,
           l_send, l_recv, local_sem):
    tile_rows, tile_cols = density.shape
    own = tile_rows // reps
    piece = own // chunks
    ratio = tile_cols // tile_rows
    z, c, p = lax.axis_index("row"), lax.axis_index("col"), lax.axis_index("rep")
    bits = []
    bit = reps // 2
    while bit:
        bits.append(bit)
        bit //= 2
    others = [lax.rem(c + step, cols) for step in range(1, cols)]

    barrier = pltpu.get_barrier_semaphore()
    for step, ok in ((1, z < rows - 1), (-1, z > 0)):
        @pl.when(ok)
        def _():
            pl.semaphore_signal(barrier, inc=1, device_id={"row": z + step}, device_id_type=MESH)
    for bit in bits:
        pl.semaphore_signal(barrier, inc=1, device_id={"rep": flip(p, bit)}, device_id_type=MESH)
    for other in others:
        pl.semaphore_signal(barrier, inc=1, device_id={"col": other}, device_id_type=MESH)
    keep_tile = pltpu.make_async_copy(
        density, panel.at[pl.ds(pl.multiple_of(z * tile_rows, tile_rows), tile_rows)], local_sem.at[0])
    keep_tile.start()
    keep_left = [
        pltpu.make_async_copy(
            density.at[pl.ds(pl.multiple_of(p * own, own), own), pl.ds(part * tile_rows, tile_rows)],
            left.at[c * ratio + part], local_sem.at[1 + part])
        for part in range(ratio)
    ]
    for copy in keep_left:
        copy.start()
    below, above = (z + rows - 1) // rows, (2 * rows - 2 - z) // rows
    pl.semaphore_wait(barrier, len(bits) + len(others) + below + above)

    def slot(t, member, q):
        return panel.at[pl.ds(pl.multiple_of(t * tile_rows + member * own + q * piece, piece), piece)]

    def packed(t, place):
        return t - (t - place - 1 + rows) // rows

    def z_copy(t, q, step, first=False, sending=True):
        at = z if sending else z - step
        source = slot(t, p, q)
        if first:
            source = density.at[pl.ds(pl.multiple_of(p * own + q * piece, piece), piece)]
        return pltpu.make_async_remote_copy(
            source, slot(t, p, q), z_send.at[t + (1 - step) // 2, q],
            z_recv.at[packed(t, at + step), q],
            device_id={"row": z + step}, device_id_type=MESH)

    def r_copies(t, q, stage):
        members = [p]
        for bit in bits[:stage]:
            members = members + [flip(member, bit) for member in members]
        peer = flip(p, bits[stage])
        base = 2 ** stage - 1
        return [
            pltpu.make_async_remote_copy(
                slot(t, member, q), slot(t, member, q), r_send.at[base + i, packed(t, z), q],
                r_recv.at[base + i, packed(t, z), q], device_id={"rep": peer}, device_id_type=MESH)
            for i, member in enumerate(members)
        ]

    def r_waits(t, q, stage):
        peer = flip(p, bits[stage])
        members = [peer]
        for bit in bits[:stage]:
            members = members + [flip(member, bit) for member in members]
        base = 2 ** stage - 1
        for i, member in enumerate(members):
            pltpu.make_async_remote_copy(
                slot(t, member, q), slot(t, member, q), r_send.at[base + i, packed(t, z), q],
                r_recv.at[base + i, packed(t, z), q], device_id={"rep": peer}, device_id_type=MESH).wait_recv()

    def a_copy(owner, peer, part):
        return pltpu.make_async_remote_copy(
            density.at[pl.ds(pl.multiple_of(p * own, own), own), pl.ds(part * tile_rows, tile_rows)],
            left.at[owner * ratio + part], a_send.at[peer, part], a_recv.at[owner, part],
            device_id={"col": peer}, device_id_type=MESH)

    def l_copy(owner, peer, part):
        return pltpu.make_async_remote_copy(
            low.at[owner * ratio + part], low.at[owner * ratio + part],
            l_send.at[peer, part], l_recv.at[owner, part],
            device_id={"col": peer}, device_id_type=MESH)

    ways = ((1, z < rows - 1), (-1, z > 0))
    for q in range(chunks):
        for step, ok in ways:
            @pl.when(ok)
            def _():
                z_copy(z, q, step, True).start()
    for other in others:
        for part in range(ratio):
            a_copy(c, other, part).start()

    def arrivals(distance):
        return ((1, z - distance, z - distance >= 0, z < rows - 1),
                (-1, z + distance, z + distance < rows, z > 0))

    def take(distance):
        for q in range(chunks):
            for step, t, ok, onward in arrivals(distance):
                @pl.when(ok)
                def _():
                    z_copy(t, q, step, sending=False).wait_recv()

                    @pl.when(onward)
                    def _():
                        z_copy(t, q, step).start()
                    for copy in r_copies(t, q, 0):
                        copy.start()

    def spread(distance, stage):
        for q in range(chunks):
            for step, t, ok, onward in arrivals(distance):
                @pl.when(ok)
                def _():
                    r_waits(t, q, stage - 1)
                    for copy in r_copies(t, q, stage):
                        copy.start()

    def product(factor, t):
        return jnp.dot(factor[t], panel[pl.ds(pl.multiple_of(t * tile_rows, tile_rows), tile_rows), :],
                       preferred_element_type=jnp.float32)

    def use(distance):
        for step, t, ok, onward in arrivals(distance):
            @pl.when(ok)
            def _():
                for q in range(chunks):
                    r_waits(t, q, len(bits) - 1)
                total[...] += product(left, t)

    keep_tile.wait()
    for copy in keep_left:
        copy.wait()
    started = False
    for distance in range(1, rows + len(bits)):
        if distance < rows:
            take(distance)
        for stage in range(1, len(bits)):
            if 1 <= distance - stage < rows:
                spread(distance - stage, stage)
        if not started:
            for other in others:
                for part in range(ratio):
                    a_copy(other, other, part).wait_recv()
            total[...] = product(left, z)
            started = True
        if 1 <= distance - len(bits) < rows:
            use(distance - len(bits))

    row_block = (p * own + lax.broadcasted_iota(jnp.int32, (own, block), 0)) // block

    def widen(keep, column):
        wide = jnp.zeros((own, block), jnp.float32)
        for i in range(tile_rows // block):
            wide = jnp.where(row_block == i, keep[i, column].astype(jnp.float32), wide)
        return wide

    per_part = tile_rows // block
    for column in range(tile_cols // block):
        span = pl.ds(column * block, block)
        square = total[:, span] * widen(keep_square, column)
        total[:, span] = square
        low[c * ratio + column // per_part, :, pl.ds(column % per_part * block, block)] = square.astype(jnp.bfloat16)
    for other in others:
        for part in range(ratio):
            l_copy(c, other, part).start()
    cube = product(low, c * ratio)
    for part in range(1, ratio):
        cube = cube + product(low, c * ratio + part)
    out[...] = cube
    for other in others:
        for part in range(ratio):
            l_copy(other, other, part).wait_recv()
            out[...] += product(low, other * ratio + part)
    for column in range(tile_cols // block):
        span = pl.ds(column * block, block)
        out[:, span] = 3.0 * total[:, span] - 2.0 * (out[:, span] * widen(keep_cube, column))

    for q in range(chunks):
        for step, ok in ways:
            @pl.when(ok)
            def _():
                z_copy(z, q, step, True).wait_send()
        for distance in range(1, rows):
            for step, t, ok, onward in arrivals(distance):
                @pl.when(ok)
                def _():
                    @pl.when(onward)
                    def _():
                        z_copy(t, q, step).wait_send()
                    for stage in range(len(bits)):
                        for copy in r_copies(t, q, stage):
                            copy.wait_send()
    for other in others:
        for part in range(ratio):
            a_copy(c, other, part).wait_send()
            l_copy(c, other, part).wait_send()


def by_panel(rows, cols, reps, mat, density, keep_square, keep_cube):
    tile_rows, tile_cols = density.shape
    block = tile_rows // keep_square.shape[0]
    own = tile_rows // reps
    ratio = tile_cols // tile_rows
    chunks = 3 if own % 48 == 0 else 1
    dma = pltpu.SemaphoreType.DMA
    return pl.pallas_call(
        functools.partial(panel_kernel, rows, cols, reps, block, chunks),
        out_shape=pltpu.VMEM((own, tile_cols), jnp.float32),
        in_specs=[
            pl.BlockSpec(memory_space=pl.ANY),
            pl.BlockSpec(memory_space=pltpu.SMEM),
            pl.BlockSpec(memory_space=pltpu.SMEM),
        ],
        out_specs=pl.BlockSpec(memory_space=pltpu.VMEM),
        scratch_shapes=[
            pltpu.VMEM((mat, tile_cols), jnp.bfloat16),
            pltpu.VMEM((rows, own, tile_rows), jnp.bfloat16),
            pltpu.VMEM((rows, own, tile_rows), jnp.bfloat16),
            pltpu.VMEM((own, tile_cols), jnp.float32),
            dma((rows + 1, chunks)),
            dma((rows - 1, chunks)),
            dma((reps - 1, rows - 1, chunks)),
            dma((reps - 1, rows - 1, chunks)),
            dma((cols, ratio)),
            dma((cols, ratio)),
            dma((cols, ratio)),
            dma((cols, ratio)),
            dma((1 + ratio,)),
        ],
        compiler_params=pltpu.CompilerParams(collective_id=0, has_side_effects=True),
    )(density, keep_square, keep_cube)


STREAMS = ("x_keep", "x_own", "y_own", "z_diag", "z_off", "y_off",
           "c_part", "x_part", "y_part", "v_part", "t_far", "t_diag", "t_off", "t_part")


def whole_kernel(reps, block, density, keep_square, keep_cube_in, out,
                 tiles, cross, corner, keeps, keep_cube, square, low, keep_wide, local_sem, ready, *sems):
    streams = {name: sems[2 * i:2 * i + 2] for i, name in enumerate(STREAMS)}
    tile, wide = density.shape
    own = tile // reps
    strips = tile // block
    sub = block // reps
    every = range(strips)
    z, c, p = lax.axis_index("row"), lax.axis_index("col"), lax.axis_index("rep")
    half, here = z // 2, z % 2
    there, other, far = 1 - here, 1 - half, 1 - c
    across = p + reps // 2 - reps * (p // (reps // 2))
    twin = p + 1 - 2 * (p % 2)
    is_diag, is_inner = c == half, here != half
    to_far, to_mate = {"col": far}, {"row": z + 1 - 2 * here}
    to_across, to_twin, to_corner = {"rep": across}, {"rep": twin}, {"col": far, "rep": across}
    quarters = (p, across)
    twins = (twin, across + 1 - 2 * (across % 2))
    distant = (3 * other, other + 1)
    near, end = 1 - other, other
    from_far, from_diag = (0, 2), (1, 3, 4, 5)

    def remote(source, target, name, index, device, arrival=None):
        send, recv = streams[name]
        return pltpu.make_async_remote_copy(
            source, target, send.at[index], recv.at[index if arrival is None else arrival],
            device_id=device, device_id_type=MESH)

    def rows(q, s):
        return pl.ds(pl.multiple_of(s * block + q * sub, sub), sub)

    def columns(start, size):
        return pl.ds(pl.multiple_of(start, block), size)

    def level_at(level):
        return columns(level * tile, tile)

    def relay(ref, name, index, device):
        return remote(ref, ref, name, index, device)

    def own_out(name, j, s, device):
        at = rows(quarters[j], s)
        return remote(density.at[at], tiles.at[c, here, at], name, j * strips + s, device)

    def tile_at(column, level, q, s):
        return tiles.at[column, level, rows(q, s)]

    def diag_at(level, q, s):
        return tiles.at[half, level, rows(q, s), columns(level * tile + s * block, tile - s * block)]

    def part_at(i, q, of=other, source=False):
        if i < strips:
            band = of * i + (1 - of) * (strips - 1 - i)
            ref = density if source else cross
            return ref.at[rows(q, band), columns(of * i * block, wide - i * block)]
        i = i - strips
        if source:
            return density.at[rows(q, i), columns(here * tile + i * block, tile - i * block)]
        return corner.at[rows(q, i), columns(i * block, tile - i * block)]

    def part_out(i, d, column):
        source = part_at(i, p, half, True)
        target = part_at(i, p, half)
        return remote(source, target, "c_part", 2 * i + d, {"row": distant[d], "col": column}, i)

    def part_in(i):
        return relay(part_at(i, p), "c_part", i, to_mate)

    def far_parts(name, i, q, device):
        return relay(part_at(i, q), name, i, device)

    def twin_part(j, i, incoming=False):
        return relay(part_at(i, (twins if incoming else quarters)[j]), "t_part", j * 2 * strips + i, to_twin)

    def twin_tile(name, column, level, j, s, incoming=False):
        return relay(tile_at(column, level, (twins if incoming else quarters)[j], s), name, j * strips + s, to_twin)

    def twin_diag(j, s, incoming=False):
        return relay(diag_at(there, (twins if incoming else quarters)[j], s), "t_diag", j * strips + s, to_twin)

    def keep_copy(at):
        return remote(keep_square, keeps.at[at], "x_keep", 0, to_far)

    def spread(i):
        part_in(i).wait_recv()
        far_parts("x_part", i, p, to_far).start()
        far_parts("y_part", i, p, to_across).start()
        far_parts("v_part", i, p, to_corner).start()
        twin_part(0, i).start()

    def gather(mine, theirs):
        for i in theirs:
            far_parts("x_part", i, p, to_far).wait_recv()
            twin_part(0, i).start()
        for i in mine:
            far_parts("y_part", i, across, to_across).wait_recv()
            twin_part(1, i).start()
        for i in theirs:
            far_parts("v_part", i, across, to_corner).wait_recv()
            twin_part(1, i).start()

    barrier = pltpu.get_barrier_semaphore()
    beside = (to_far, to_mate, to_across, to_twin, to_corner)
    for device in beside:
        pl.semaphore_signal(barrier, inc=1, device_id=device, device_id_type=MESH)
    is_low = half == 0

    @pl.when(is_low)
    def _():
        for at in distant:
            pl.semaphore_signal(barrier, inc=1, device_id={"row": at, "col": other}, device_id_type=MESH)

    @pl.when(is_low & is_diag)
    def _():
        for at in distant:
            for column in (c, far):
                pl.semaphore_signal(barrier, inc=1, device_id={"row": at, "col": column}, device_id_type=MESH)

    tile_copy = pltpu.make_async_copy(density, tiles.at[c, here], local_sem.at[0])
    tile_copy.start()
    keep_local = pltpu.make_async_copy(keep_square, keeps.at[c], local_sem.at[1])
    keep_local.start()
    keep_cube_copy = pltpu.make_async_copy(keep_cube_in, keep_cube, local_sem.at[2])
    keep_cube_copy.start()

    row_block = (p * own + lax.broadcasted_iota(jnp.int32, (own, block), 0)) // block

    def widen(at, keep, scale):
        for column in range(wide // block):
            value = jnp.zeros((own, block), jnp.float32)
            for i in range(tile // block):
                value = jnp.where(row_block == i, keep(i, column).astype(jnp.float32) * scale, value)
            keep_wide[at, :, pl.ds(column * block, block)] = value

    def parts_out(done=False):
        for d in range(2):
            @pl.when(is_inner)
            def _():
                for i in (1, 0, 2):
                    copy = part_out(i, d, far if i in from_diag else c)
                    copy.wait_send() if done else copy.start()

            @pl.when(jnp.logical_not(is_inner))
            def _():
                for i in range(strips, 2 * strips):
                    copy = part_out(i, d, far)
                    copy.wait_send() if done else copy.start()

    @pl.when(is_low)
    def _():
        pl.semaphore_wait(barrier, len(beside))

    @pl.when(jnp.logical_not(is_low))
    def _():
        @pl.when(is_diag)
        def _():
            pl.semaphore_wait(barrier, len(beside) + 6)
            parts_out()

        @pl.when(jnp.logical_not(is_diag))
        def _():
            pl.semaphore_wait(barrier, len(beside) + 2)
        for at in distant:
            pl.semaphore_signal(ready, inc=1, device_id={"row": at, "col": other}, device_id_type=MESH)

    keep_copy(c).start()
    for s in every:
        own_out("x_own", 0, s, to_far).start()

    @pl.when(is_diag)
    def _():
        for s in every:
            own_out("x_own", 1, s, to_far).start()
        for j in range(2):
            for s in every:
                remote(density.at[rows(quarters[j], s), columns(here * tile + s * block, tile - s * block)],
                       diag_at(here, quarters[j], s), "z_diag", j * strips + s, to_mate).start()

        for s in every:
            relay(tile_at(other, here, p, s), "x_own", s, to_far).wait_recv()
            if s == 0:
                @pl.when(is_low)
                def _():
                    pl.semaphore_wait(ready, 4)
                    parts_out()
            relay(tile_at(other, here, p, s), "y_own", s, to_across).start()
            relay(tile_at(other, here, p, s), "z_off", s, to_mate).start()
            twin_tile("t_far", other, here, 0, s).start()

        for j in range(2):
            for s in every:
                relay(diag_at(there, quarters[j], s), "z_diag", j * strips + s, to_mate).wait_recv()
                twin_diag(j, s).start()
        for s in every:
            relay(tile_at(other, here, across, s), "y_own", s, to_across).wait_recv()
            relay(tile_at(other, here, across, s), "z_off", strips + s, to_mate).start()
            twin_tile("t_far", other, here, 1, s).start()
        for i in from_diag:
            spread(i)
        for s in every:
            relay(tile_at(other, there, p, s), "z_off", s, to_mate).wait_recv()
            twin_tile("t_off", other, there, 0, s).start()

    @pl.when(jnp.logical_not(is_diag))
    def _():
        for s in every:
            own_out("z_off", 0, s, to_mate).start()
        for s in every:
            relay(tile_at(other, there, p, s), "z_off", s, to_mate).wait_recv()
            relay(tile_at(other, there, p, s), "y_off", s, to_across).start()
            twin_tile("t_off", other, there, 0, s).start()
        def pass_far(j):
            for s in every:
                relay(tile_at(half, here, quarters[j], s), "x_own", j * strips + s, to_far).wait_recv()
                relay(diag_at(here, quarters[j], s), "z_diag", j * strips + s, to_mate).start()
                twin_tile("t_far", half, here, j, s).start()

        pass_far(0)
        for i in from_far:
            spread(i)
        pass_far(1)
        for s in every:
            relay(tile_at(other, there, across, s), "y_off", s, to_across).wait_recv()
            twin_tile("t_off", other, there, 1, s).start()
        for j in range(2):
            for s in every:
                relay(diag_at(there, quarters[j], s), "z_diag", j * strips + s, to_mate).wait_recv()
                twin_diag(j, s).start()

    tile_copy.wait()
    keep_cube_copy.wait()
    widen(2, lambda i, j: keep_cube[i, j], -2.0)
    keep_local.wait()
    widen(c, lambda i, j: keeps[c, i, j], 1.0)
    keep_copy(far).wait_recv()
    widen(far, lambda i, j: keeps[far, i, j], 1.0)

    def dot(a, b, contract=0):
        return lax.dot_general(a, b, (((1,), (contract,)), ((), ())), preferred_element_type=jnp.float32)

    def complete(ref, lead, level, source_first):
        for a in every:
            for b in range(a + 1, strips):
                r, t = (a, b) if source_first is None else (b + source_first * (a - b), a + source_first * (b - a))
                block_at = lambda i, j: lead + (columns(i * block, block), columns(level * tile + j * block, block))
                ref[block_at(t, r)] = ref[block_at(r, t)].T

    def by_diag(left_here, left_there):
        a = tiles[half, here, :, level_at(here)]
        b = tiles[half, here, :, level_at(there)]
        d = tiles[half, there, :, level_at(there)]
        return dot(left_here, a) + dot(left_there, b, 1), dot(left_here, b) + dot(left_there, d)

    def by_cross(left_near, left_end):
        a = cross[:, level_at(near)]
        b = cross[:, level_at(end)]
        return dot(left_near, a) + dot(left_end, b, 1), dot(left_near, b) + dot(left_end, corner[...])

    my_rows = pl.ds(pl.multiple_of(p * own, own), own)

    for j in range(2):
        for s in every:
            twin_diag(j, s, True).wait_recv()
            twin_tile("t_far", far, here, j, s, True).wait_recv()
    complete(tiles, (half, there), there, None)
    lh = [tiles[half, here, my_rows, level_at(level)] for level in (here, there)]
    lo = tiles[other, here, my_rows, :]
    h_here, h_there = by_diag(*lh)
    square[half, :, level_at(here)] = h_here + dot(lo, tiles[other, here], 1)
    square[half, :, level_at(there)] = h_there
    square[other] = dot(lh[0], tiles[other, here])

    @pl.when(is_diag)
    def _():
        gather(from_diag, from_far)
        for s in every:
            relay(tile_at(other, there, across, s), "z_off", strips + s, to_mate).wait_recv()
            twin_tile("t_off", other, there, 1, s).start()

    for j in range(2):
        for s in every:
            twin_tile("t_off", other, there, j, s, True).wait_recv()

    def mask(at):
        value = square[at] * keep_wide[at]
        square[at] = value
        low[at] = value.astype(jnp.bfloat16)

    square[half, :, level_at(there)] += dot(lo, tiles[other, there], 1)
    mask(half)
    square[other] += dot(lh[1], tiles[other, there])

    @pl.when(is_diag)
    def _():
        h_here, h_there = by_diag(low[half, :, level_at(here)], low[half, :, level_at(there)])
        out[:, level_at(here)] = h_here
        out[:, level_at(there)] = h_there

    @pl.when(jnp.logical_not(is_diag))
    def _():
        gather(from_far, from_diag)
        out[...] = (dot(low[half, :, level_at(here)], tiles[other, here])
                    + dot(low[half, :, level_at(there)], tiles[other, there]))

    for j in range(2):
        for i in range(2 * strips):
            twin_part(j, i, True).wait_recv()
    complete(cross, (), near, other)
    complete(corner, (), 0, None)
    o_near, o_end = by_cross(*(tiles[other, here, my_rows, level_at(level)] for level in (near, end)))
    square[other, :, level_at(near)] += o_near
    square[other, :, level_at(end)] += o_end
    mask(other)

    @pl.when(is_diag)
    def _():
        for level in (here, there):
            span = level_at(level)
            cube = out[:, span] + dot(low[other], tiles[other, level], 1)
            out[:, span] = 3.0 * square[c, :, span] + cube * keep_wide[2, :, span]

    @pl.when(jnp.logical_not(is_diag))
    def _():
        cubes = by_cross(low[other, :, level_at(near)], low[other, :, level_at(end)])
        for level, part in zip((near, end), cubes):
            span = level_at(level)
            cube = out[:, span] + part
            out[:, span] = 3.0 * square[c, :, span] + cube * keep_wide[2, :, span]

    keep_copy(c).wait_send()
    for s in every:
        own_out("x_own", 0, s, to_far).wait_send()
        for j in range(2):
            relay(diag_at(here, quarters[j], s), "z_diag", j * strips + s, to_mate).wait_send()
            twin_tile("t_far", far, here, j, s).wait_send()
            twin_tile("t_off", other, there, j, s).wait_send()
            twin_diag(j, s).wait_send()
    for j in range(2):
        for i in range(2 * strips):
            twin_part(j, i).wait_send()

    def spread_sent(mine):
        for i in mine:
            far_parts("x_part", i, p, to_far).wait_send()
            far_parts("y_part", i, p, to_across).wait_send()
            far_parts("v_part", i, p, to_corner).wait_send()

    @pl.when(is_diag)
    def _():
        spread_sent(from_diag)
        parts_out(done=True)
        for s in every:
            own_out("x_own", 1, s, to_far).wait_send()
            relay(tile_at(other, here, p, s), "y_own", s, to_across).wait_send()
            for j in range(2):
                relay(tile_at(other, here, quarters[j], s), "z_off", j * strips + s, to_mate).wait_send()

    @pl.when(jnp.logical_not(is_diag))
    def _():
        spread_sent(from_far)
        for s in every:
            own_out("z_off", 0, s, to_mate).wait_send()
            relay(tile_at(other, there, p, s), "y_off", s, to_across).wait_send()


def by_whole(reps, density, keep_square, keep_cube):
    tile, wide = density.shape
    block = tile // keep_square.shape[0]
    own = tile // reps
    strips = tile // block
    dma = pltpu.SemaphoreType.DMA
    low = jnp.bfloat16
    return pl.pallas_call(
        functools.partial(whole_kernel, reps, block),
        out_shape=pltpu.VMEM((own, wide), jnp.float32),
        in_specs=[
            pl.BlockSpec(memory_space=pl.ANY),
            pl.BlockSpec(memory_space=pl.ANY),
            pl.BlockSpec(memory_space=pl.ANY),
        ],
        out_specs=pl.BlockSpec(memory_space=pltpu.VMEM),
        scratch_shapes=[
            pltpu.VMEM((2, 2, tile, wide), low),
            pltpu.VMEM((tile, wide), low),
            pltpu.VMEM((tile, tile), low),
            pltpu.SMEM((2,) + keep_square.shape, jnp.int32),
            pltpu.SMEM(keep_cube.shape, jnp.int32),
            pltpu.VMEM((2, own, wide), jnp.float32),
            pltpu.VMEM((2, own, wide), low),
            pltpu.VMEM((3, own, wide), jnp.float32),
            dma((3,)),
            pltpu.SemaphoreType.REGULAR,
        ] + [dma((4 * strips,))] * (2 * len(STREAMS)),
        compiler_params=pltpu.CompilerParams(collective_id=0, has_side_effects=True),
    )(density, keep_square, keep_cube)


def solution(mesh):
    rows, cols, reps = (mesh.shape[axis] for axis in ("row", "col", "rep"))

    def body(density, keep_square, keep_cube):
        tile, wide = density.shape
        if cols == 2 and rows == 2 * cols and reps == 4 and tile * rows == wide * cols:
            return by_whole(reps, density, keep_square, keep_cube)
        return by_panel(rows, cols, reps, tile * rows, density, keep_square, keep_cube)

    return jax.shard_map(
        body,
        mesh=mesh,
        in_specs=(P("row", "col"), P("row", "col"), P("row", "col")),
        out_specs=P(("row", "rep"), "col"),
        check_vma=False,
    )
```

```python
import functools

import jax
import jax.numpy as jnp
from jax import lax
from jax.experimental import pallas as pl
from jax.experimental.pallas import tpu as pltpu
from jax.sharding import PartitionSpec as P

MESH = pl.DeviceIdType.MESH

def flip(index, bit):
    return index + bit - 2 * bit * (index // bit % 2)


def panel_kernel(rows, cols, reps, block, chunks, density, keep_square, keep_cube, out,
           panel, left, low, total, z_send, z_recv, r_send, r_recv, a_send, a_recv,
           l_send, l_recv, local_sem):
    tile_rows, tile_cols = density.shape
    own = tile_rows // reps
    piece = own // chunks
    ratio = tile_cols // tile_rows
    z, c, p = lax.axis_index("row"), lax.axis_index("col"), lax.axis_index("rep")
    bits = []
    bit = reps // 2
    while bit:
        bits.append(bit)
        bit //= 2
    others = [lax.rem(c + step, cols) for step in range(1, cols)]

    barrier = pltpu.get_barrier_semaphore()
    for step, ok in ((1, z < rows - 1), (-1, z > 0)):
        @pl.when(ok)
        def _():
            pl.semaphore_signal(barrier, inc=1, device_id={"row": z + step}, device_id_type=MESH)
    for bit in bits:
        pl.semaphore_signal(barrier, inc=1, device_id={"rep": flip(p, bit)}, device_id_type=MESH)
    for other in others:
        pl.semaphore_signal(barrier, inc=1, device_id={"col": other}, device_id_type=MESH)
    keep_tile = pltpu.make_async_copy(
        density, panel.at[pl.ds(pl.multiple_of(z * tile_rows, tile_rows), tile_rows)], local_sem.at[0])
    keep_tile.start()
    keep_left = [
        pltpu.make_async_copy(
            density.at[pl.ds(pl.multiple_of(p * own, own), own), pl.ds(part * tile_rows, tile_rows)],
            left.at[c * ratio + part], local_sem.at[1 + part])
        for part in range(ratio)
    ]
    for copy in keep_left:
        copy.start()
    below, above = (z + rows - 1) // rows, (2 * rows - 2 - z) // rows
    pl.semaphore_wait(barrier, len(bits) + len(others) + below + above)

    def slot(t, member, q):
        return panel.at[pl.ds(pl.multiple_of(t * tile_rows + member * own + q * piece, piece), piece)]

    def packed(t, place):
        return t - (t - place - 1 + rows) // rows

    def z_copy(t, q, step, first=False, sending=True):
        at = z if sending else z - step
        source = slot(t, p, q)
        if first:
            source = density.at[pl.ds(pl.multiple_of(p * own + q * piece, piece), piece)]
        return pltpu.make_async_remote_copy(
            source, slot(t, p, q), z_send.at[t + (1 - step) // 2, q],
            z_recv.at[packed(t, at + step), q],
            device_id={"row": z + step}, device_id_type=MESH)

    def r_copies(t, q, stage):
        members = [p]
        for bit in bits[:stage]:
            members = members + [flip(member, bit) for member in members]
        peer = flip(p, bits[stage])
        base = 2 ** stage - 1
        return [
            pltpu.make_async_remote_copy(
                slot(t, member, q), slot(t, member, q), r_send.at[base + i, packed(t, z), q],
                r_recv.at[base + i, packed(t, z), q], device_id={"rep": peer}, device_id_type=MESH)
            for i, member in enumerate(members)
        ]

    def r_waits(t, q, stage):
        peer = flip(p, bits[stage])
        members = [peer]
        for bit in bits[:stage]:
            members = members + [flip(member, bit) for member in members]
        base = 2 ** stage - 1
        for i, member in enumerate(members):
            pltpu.make_async_remote_copy(
                slot(t, member, q), slot(t, member, q), r_send.at[base + i, packed(t, z), q],
                r_recv.at[base + i, packed(t, z), q], device_id={"rep": peer}, device_id_type=MESH).wait_recv()

    def a_copy(owner, peer, part):
        return pltpu.make_async_remote_copy(
            density.at[pl.ds(pl.multiple_of(p * own, own), own), pl.ds(part * tile_rows, tile_rows)],
            left.at[owner * ratio + part], a_send.at[peer, part], a_recv.at[owner, part],
            device_id={"col": peer}, device_id_type=MESH)

    def l_copy(owner, peer, part):
        return pltpu.make_async_remote_copy(
            low.at[owner * ratio + part], low.at[owner * ratio + part],
            l_send.at[peer, part], l_recv.at[owner, part],
            device_id={"col": peer}, device_id_type=MESH)

    ways = ((1, z < rows - 1), (-1, z > 0))
    for q in range(chunks):
        for step, ok in ways:
            @pl.when(ok)
            def _():
                z_copy(z, q, step, True).start()
    for other in others:
        for part in range(ratio):
            a_copy(c, other, part).start()

    def arrivals(distance):
        return ((1, z - distance, z - distance >= 0, z < rows - 1),
                (-1, z + distance, z + distance < rows, z > 0))

    def take(distance):
        for q in range(chunks):
            for step, t, ok, onward in arrivals(distance):
                @pl.when(ok)
                def _():
                    z_copy(t, q, step, sending=False).wait_recv()

                    @pl.when(onward)
                    def _():
                        z_copy(t, q, step).start()
                    for copy in r_copies(t, q, 0):
                        copy.start()

    def spread(distance, stage):
        for q in range(chunks):
            for step, t, ok, onward in arrivals(distance):
                @pl.when(ok)
                def _():
                    r_waits(t, q, stage - 1)
                    for copy in r_copies(t, q, stage):
                        copy.start()

    def product(factor, t):
        return jnp.dot(factor[t], panel[pl.ds(pl.multiple_of(t * tile_rows, tile_rows), tile_rows), :],
                       preferred_element_type=jnp.float32)

    def use(distance):
        for step, t, ok, onward in arrivals(distance):
            @pl.when(ok)
            def _():
                for q in range(chunks):
                    r_waits(t, q, len(bits) - 1)
                total[...] += product(left, t)

    keep_tile.wait()
    for copy in keep_left:
        copy.wait()
    started = False
    for distance in range(1, rows + len(bits)):
        if distance < rows:
            take(distance)
        for stage in range(1, len(bits)):
            if 1 <= distance - stage < rows:
                spread(distance - stage, stage)
        if not started:
            for other in others:
                for part in range(ratio):
                    a_copy(other, other, part).wait_recv()
            total[...] = product(left, z)
            started = True
        if 1 <= distance - len(bits) < rows:
            use(distance - len(bits))

    row_block = (p * own + lax.broadcasted_iota(jnp.int32, (own, block), 0)) // block

    def widen(keep, column):
        wide = jnp.zeros((own, block), jnp.float32)
        for i in range(tile_rows // block):
            wide = jnp.where(row_block == i, keep[i, column].astype(jnp.float32), wide)
        return wide

    per_part = tile_rows // block
    for column in range(tile_cols // block):
        span = pl.ds(column * block, block)
        square = total[:, span] * widen(keep_square, column)
        total[:, span] = square
        low[c * ratio + column // per_part, :, pl.ds(column % per_part * block, block)] = square.astype(jnp.bfloat16)
    for other in others:
        for part in range(ratio):
            l_copy(c, other, part).start()
    cube = product(low, c * ratio)
    for part in range(1, ratio):
        cube = cube + product(low, c * ratio + part)
    out[...] = cube
    for other in others:
        for part in range(ratio):
            l_copy(other, other, part).wait_recv()
            out[...] += product(low, other * ratio + part)
    for column in range(tile_cols // block):
        span = pl.ds(column * block, block)
        out[:, span] = 3.0 * total[:, span] - 2.0 * (out[:, span] * widen(keep_cube, column))

    for q in range(chunks):
        for step, ok in ways:
            @pl.when(ok)
            def _():
                z_copy(z, q, step, True).wait_send()
        for distance in range(1, rows):
            for step, t, ok, onward in arrivals(distance):
                @pl.when(ok)
                def _():
                    @pl.when(onward)
                    def _():
                        z_copy(t, q, step).wait_send()
                    for stage in range(len(bits)):
                        for copy in r_copies(t, q, stage):
                            copy.wait_send()
    for other in others:
        for part in range(ratio):
            a_copy(c, other, part).wait_send()
            l_copy(c, other, part).wait_send()


def by_panel(rows, cols, reps, mat, density, keep_square, keep_cube):
    tile_rows, tile_cols = density.shape
    block = tile_rows // keep_square.shape[0]
    own = tile_rows // reps
    ratio = tile_cols // tile_rows
    chunks = 3 if own % 48 == 0 else 1
    dma = pltpu.SemaphoreType.DMA
    return pl.pallas_call(
        functools.partial(panel_kernel, rows, cols, reps, block, chunks),
        out_shape=pltpu.VMEM((own, tile_cols), jnp.float32),
        in_specs=[
            pl.BlockSpec(memory_space=pl.ANY),
            pl.BlockSpec(memory_space=pltpu.SMEM),
            pl.BlockSpec(memory_space=pltpu.SMEM),
        ],
        out_specs=pl.BlockSpec(memory_space=pltpu.VMEM),
        scratch_shapes=[
            pltpu.VMEM((mat, tile_cols), jnp.bfloat16),
            pltpu.VMEM((rows, own, tile_rows), jnp.bfloat16),
            pltpu.VMEM((rows, own, tile_rows), jnp.bfloat16),
            pltpu.VMEM((own, tile_cols), jnp.float32),
            dma((rows + 1, chunks)),
            dma((rows - 1, chunks)),
            dma((reps - 1, rows - 1, chunks)),
            dma((reps - 1, rows - 1, chunks)),
            dma((cols, ratio)),
            dma((cols, ratio)),
            dma((cols, ratio)),
            dma((cols, ratio)),
            dma((1 + ratio,)),
        ],
        compiler_params=pltpu.CompilerParams(collective_id=0, has_side_effects=True),
    )(density, keep_square, keep_cube)


ARRIVALS = {"x_keep": 1, "x_own": 4, "y_own": 3, "z_diag": 1, "z_off": 4, "y_off": 1, "c_part": 4, "x_part": 4,
            "y_part": 4, "v_part": 4, "t_far": 1, "t_diag": 1, "t_off": 1, "t_part": 1}
SENDS = {"x_keep": 0, "x_own": 1, "y_own": 1, "z_diag": 2, "z_off": 2, "y_off": 2, "c_part": 3, "x_part": 3,
         "y_part": 3, "v_part": 3, "t_far": 4, "t_off": 4, "t_diag": 5, "t_part": 5}


def whole_kernel(reps, block, density, keep_square, keep_cube_in, out,
                 tiles, cross, corner, keeps, keep_cube, square, low, keep_wide, local_sem, ready, sends, *sems):
    arrivals = dict(zip(ARRIVALS, sems))
    tile, wide = density.shape
    own = tile // reps
    strips = tile // block
    sub = block // reps
    every = range(strips)
    z, c, p = lax.axis_index("row"), lax.axis_index("col"), lax.axis_index("rep")
    half, here = z // 2, z % 2
    there, other, far = 1 - here, 1 - half, 1 - c
    across = p + reps // 2 - reps * (p // (reps // 2))
    twin = p + 1 - 2 * (p % 2)
    is_diag, is_inner = c == half, here != half
    to_far, to_mate = {"col": far}, {"row": z + 1 - 2 * here}
    to_across, to_twin, to_corner = {"rep": across}, {"rep": twin}, {"col": far, "rep": across}
    quarters = (p, across)
    twins = (twin, across + 1 - 2 * (across % 2))
    distant = (3 * other, other + 1)
    near, end = 1 - other, other
    from_far, from_diag = (0, 2), (1, 3)

    def remote(source, target, name, index, device):
        return pltpu.make_async_remote_copy(
            source, target, sends.at[SENDS[name]], arrivals[name].at[index], device_id=device, device_id_type=MESH)

    def bulk(width):
        blocks = width * sub // block
        many = next(m for m in range(wide // block, 0, -1)
                    if blocks % (16 * m) == 0 and blocks // m <= tile)
        return cross.at[pl.ds(0, blocks // many), pl.ds(0, many * block)]

    def arrived(name, index, width):
        ref = bulk(width)
        remote(ref, ref, name, index, to_mate).wait_recv()

    def sent(name, width):
        ref = bulk(width)
        remote(ref, ref, name, 0, to_mate).wait_send()

    def rows(q, s):
        return pl.ds(pl.multiple_of(s * block + q * sub, sub), sub)

    def columns(start, size):
        return pl.ds(pl.multiple_of(start, block), size)

    def level_at(level):
        return columns(level * tile, tile)

    def relay(ref, name, index, device):
        return remote(ref, ref, name, index, device)

    def own_out(name, j, s, device):
        at = rows(quarters[j], s)
        index = s if j == 0 else strips
        return remote(density.at[at], tiles.at[c, here, at], name, index, device)

    def tile_at(column, level, q, s):
        return tiles.at[column, level, rows(q, s)]

    def diag_at(level, q, s):
        return tiles.at[half, level, rows(q, s), columns(level * tile + s * block, tile - s * block)]

    def part_at(i, q, of=other, source=False):
        if i < strips:
            band = of * i + (1 - of) * (strips - 1 - i)
            ref = density if source else cross
            return [ref.at[rows(q, band), columns(of * i * block, wide - i * block)]]
        if source:
            return [density.at[rows(q, s), columns(here * tile + s * block, tile - s * block)] for s in every]
        return [corner.at[rows(q, s), columns(s * block, tile - s * block)] for s in every]

    triangle = sum(tile - s * block for s in every)
    part_width = [wide - s * block for s in every] + [triangle]

    def part_out(i, d, column):
        for source, target in zip(part_at(i, p, half, True), part_at(i, p, half)):
            remote(source, target, "c_part", i, {"row": distant[d], "col": column}).start()

    def part_on(name, i, q, device, index=None):
        for ref in part_at(i, q):
            relay(ref, name, i if index is None else index, device).start()

    def twin_part(j, i):
        part_on("t_part", i, quarters[j], to_twin, 0)

    def twin_tile(name, column, level, j, s):
        relay(tile_at(column, level, quarters[j], s), name, 0, to_twin).start()

    def twin_diag(j):
        for s in every:
            relay(diag_at(there, quarters[j], s), "t_diag", 0, to_twin).start()

    def keep_copy(at):
        return remote(keep_square, keeps.at[at], "x_keep", 0, to_far)

    def spread(i):
        arrived("c_part", i, part_width[i])
        part_on("x_part", i, p, to_far)
        part_on("v_part", i, p, to_corner)
        part_on("y_part", i, p, to_across)
        twin_part(0, i)

    def gather(mine, theirs):
        for i in theirs:
            arrived("x_part", i, part_width[i])
            twin_part(0, i)
        for i in mine:
            arrived("y_part", i, part_width[i])
            twin_part(1, i)
        for i in theirs:
            arrived("v_part", i, part_width[i])
            twin_part(1, i)

    barrier = pltpu.get_barrier_semaphore()
    beside = (to_far, to_mate, to_across, to_twin, to_corner)
    for device in beside:
        pl.semaphore_signal(barrier, inc=1, device_id=device, device_id_type=MESH)
    is_low = half == 0

    @pl.when(is_low)
    def _():
        for at in distant:
            pl.semaphore_signal(barrier, inc=1, device_id={"row": at, "col": other}, device_id_type=MESH)

    @pl.when(is_low & is_diag)
    def _():
        for at in distant:
            for column in (c, far):
                pl.semaphore_signal(barrier, inc=1, device_id={"row": at, "col": column}, device_id_type=MESH)

    tile_copy = pltpu.make_async_copy(density, tiles.at[c, here], local_sem.at[0])
    tile_copy.start()
    keep_local = pltpu.make_async_copy(keep_square, keeps.at[c], local_sem.at[1])
    keep_local.start()
    keep_cube_copy = pltpu.make_async_copy(keep_cube_in, keep_cube, local_sem.at[2])
    keep_cube_copy.start()

    row_block = (p * own + lax.broadcasted_iota(jnp.int32, (own, block), 0)) // block

    def widen(at, keep, scale):
        for column in range(wide // block):
            value = jnp.zeros((own, block), jnp.float32)
            for i in range(tile // block):
                value = jnp.where(row_block == i, keep(i, column).astype(jnp.float32) * scale, value)
            keep_wide[at, :, pl.ds(column * block, block)] = value

    def parts_out():
        for d in range(2):
            @pl.when(is_inner)
            def _():
                for i in (1, 0, 2):
                    part_out(i, d, far if i in from_diag else c)

            @pl.when(jnp.logical_not(is_inner))
            def _():
                part_out(strips, d, far)

    @pl.when(is_low)
    def _():
        pl.semaphore_wait(barrier, len(beside))

    @pl.when(jnp.logical_not(is_low))
    def _():
        @pl.when(is_diag)
        def _():
            pl.semaphore_wait(barrier, len(beside) + 6)
            parts_out()

        @pl.when(jnp.logical_not(is_diag))
        def _():
            pl.semaphore_wait(barrier, len(beside) + 2)
        for at in distant:
            pl.semaphore_signal(ready, inc=1, device_id={"row": at, "col": other}, device_id_type=MESH)

    keep_copy(c).start()
    for s in every:
        own_out("x_own", 0, s, to_far).start()

    @pl.when(is_diag)
    def _():
        for s in every:
            own_out("x_own", 1, s, to_far).start()
        for j in range(2):
            for s in every:
                remote(density.at[rows(quarters[j], s), columns(here * tile + s * block, tile - s * block)],
                       diag_at(here, quarters[j], s), "z_diag", 0, to_mate).start()

        for s in every:
            arrived("x_own", s, wide)
            if s == 0:
                @pl.when(is_low)
                def _():
                    pl.semaphore_wait(ready, 4)
                    parts_out()
            relay(tile_at(other, here, p, s), "y_own", s, to_across).start()
            relay(tile_at(other, here, p, s), "z_off", s, to_mate).start()
            twin_tile("t_far", other, here, 0, s)
        arrived("z_diag", 0, 2 * triangle)
        for j in range(2):
            twin_diag(j)
        for s in every:
            arrived("y_own", s, wide)
            relay(tile_at(other, here, across, s), "z_off", strips, to_mate).start()
            twin_tile("t_far", other, here, 1, s)
        for i in from_diag:
            spread(i)
        for s in every:
            arrived("z_off", s, wide)
            twin_tile("t_off", other, there, 0, s)

    @pl.when(jnp.logical_not(is_diag))
    def _():
        for s in every:
            own_out("z_off", 0, s, to_mate).start()
        for s in every:
            arrived("z_off", s, wide)
            relay(tile_at(other, there, p, s), "y_off", 0, to_across).start()
            twin_tile("t_off", other, there, 0, s)

        def pass_far(j, s):
            relay(diag_at(here, quarters[j], s), "z_diag", 0, to_mate).start()
            twin_tile("t_far", half, here, j, s)

        for s in every:
            arrived("x_own", s, wide)
            pass_far(0, s)
        for i in from_far:
            spread(i)
        arrived("x_own", strips, strips * wide)
        for s in every:
            pass_far(1, s)
        arrived("y_off", 0, strips * wide)
        for s in every:
            twin_tile("t_off", other, there, 1, s)
        arrived("z_diag", 0, 2 * triangle)
        for j in range(2):
            twin_diag(j)

    tile_copy.wait()
    keep_cube_copy.wait()
    widen(2, lambda i, j: keep_cube[i, j], -2.0)
    keep_local.wait()
    widen(c, lambda i, j: keeps[c, i, j], 1.0)
    keep_copy(far).wait_recv()
    widen(far, lambda i, j: keeps[far, i, j], 1.0)

    def dot(a, b, contract=0):
        return lax.dot_general(a, b, (((1,), (contract,)), ((), ())), preferred_element_type=jnp.float32)

    def complete(ref, lead, level, source_first):
        for a in every:
            for b in range(a + 1, strips):
                r, t = (a, b) if source_first is None else (b + source_first * (a - b), a + source_first * (b - a))
                block_at = lambda i, j: lead + (columns(i * block, block), columns(level * tile + j * block, block))
                ref[block_at(t, r)] = ref[block_at(r, t)].T

    def by_diag(left_here, left_there):
        a = tiles[half, here, :, level_at(here)]
        b = tiles[half, here, :, level_at(there)]
        d = tiles[half, there, :, level_at(there)]
        return dot(left_here, a) + dot(left_there, b, 1), dot(left_here, b) + dot(left_there, d)

    def by_cross(left_near, left_end):
        a = cross[:, level_at(near)]
        b = cross[:, level_at(end)]
        return dot(left_near, a) + dot(left_end, b, 1), dot(left_near, b) + dot(left_end, corner[...])

    my_rows = pl.ds(pl.multiple_of(p * own, own), own)

    arrived("t_diag", 0, 2 * triangle)
    arrived("t_far", 0, 2 * strips * wide)
    complete(tiles, (half, there), there, None)
    lh = [tiles[half, here, my_rows, level_at(level)] for level in (here, there)]
    lo = tiles[other, here, my_rows, :]
    h_here, h_there = by_diag(*lh)
    square[half, :, level_at(here)] = h_here + dot(lo, tiles[other, here], 1)
    square[half, :, level_at(there)] = h_there
    square[other] = dot(lh[0], tiles[other, here])

    @pl.when(is_diag)
    def _():
        gather(from_diag, from_far)
        arrived("z_off", strips, strips * wide)
        for s in every:
            twin_tile("t_off", other, there, 1, s)

    arrived("t_off", 0, 2 * strips * wide)

    def mask(at):
        value = square[at] * keep_wide[at]
        square[at] = value
        low[at] = value.astype(jnp.bfloat16)

    square[half, :, level_at(there)] += dot(lo, tiles[other, there], 1)
    mask(half)
    square[other] += dot(lh[1], tiles[other, there])

    @pl.when(is_diag)
    def _():
        h_here, h_there = by_diag(low[half, :, level_at(here)], low[half, :, level_at(there)])
        out[:, level_at(here)] = h_here
        out[:, level_at(there)] = h_there

    @pl.when(jnp.logical_not(is_diag))
    def _():
        gather(from_far, from_diag)
        out[...] = (dot(low[half, :, level_at(here)], tiles[other, here])
                    + dot(low[half, :, level_at(there)], tiles[other, there]))

    arrived("t_part", 0, 2 * sum(part_width))
    complete(cross, (), near, other)
    complete(corner, (), 0, None)
    o_near, o_end = by_cross(*(tiles[other, here, my_rows, level_at(level)] for level in (near, end)))
    square[other, :, level_at(near)] += o_near
    square[other, :, level_at(end)] += o_end
    mask(other)

    @pl.when(is_diag)
    def _():
        for level in (here, there):
            span = level_at(level)
            cube = out[:, span] + dot(low[other], tiles[other, level], 1)
            out[:, span] = 3.0 * square[c, :, span] + cube * keep_wide[2, :, span]

    @pl.when(jnp.logical_not(is_diag))
    def _():
        cubes = by_cross(low[other, :, level_at(near)], low[other, :, level_at(end)])
        for level, part in zip((near, end), cubes):
            span = level_at(level)
            cube = out[:, span] + part
            out[:, span] = 3.0 * square[c, :, span] + cube * keep_wide[2, :, span]

    keep_copy(c).wait_send()
    sent("t_off", 4 * strips * wide)
    sent("t_part", 2 * triangle + 2 * sum(part_width))

    @pl.when(is_diag)
    def _():
        sent("x_own", 3 * strips * wide)
        sent("z_off", 2 * strips * wide + 2 * triangle)
        onward = 3 * sum(part_width[i] for i in from_diag)

        @pl.when(is_inner)
        def _():
            sent("c_part", onward + 2 * sum(part_width[:strips]))

        @pl.when(jnp.logical_not(is_inner))
        def _():
            sent("c_part", onward + 2 * triangle)

    @pl.when(jnp.logical_not(is_diag))
    def _():
        sent("x_own", strips * wide)
        sent("z_off", 2 * strips * wide + 2 * triangle)
        sent("c_part", 3 * sum(part_width[i] for i in from_far))


def by_whole(reps, density, keep_square, keep_cube):
    tile, wide = density.shape
    block = tile // keep_square.shape[0]
    own = tile // reps
    strips = tile // block
    dma = pltpu.SemaphoreType.DMA
    low = jnp.bfloat16
    return pl.pallas_call(
        functools.partial(whole_kernel, reps, block),
        out_shape=pltpu.VMEM((own, wide), jnp.float32),
        in_specs=[
            pl.BlockSpec(memory_space=pl.ANY),
            pl.BlockSpec(memory_space=pl.ANY),
            pl.BlockSpec(memory_space=pl.ANY),
        ],
        out_specs=pl.BlockSpec(memory_space=pltpu.VMEM),
        scratch_shapes=[
            pltpu.VMEM((2, 2, tile, wide), low),
            pltpu.VMEM((tile, wide), low),
            pltpu.VMEM((tile, tile), low),
            pltpu.SMEM((2,) + keep_square.shape, jnp.int32),
            pltpu.SMEM(keep_cube.shape, jnp.int32),
            pltpu.VMEM((2, own, wide), jnp.float32),
            pltpu.VMEM((2, own, wide), low),
            pltpu.VMEM((3, own, wide), jnp.float32),
            dma((3,)),
            pltpu.SemaphoreType.REGULAR,
            dma((max(SENDS.values()) + 1,)),
        ] + [dma((count,)) for count in ARRIVALS.values()],
        compiler_params=pltpu.CompilerParams(collective_id=0, has_side_effects=True),
    )(density, keep_square, keep_cube)


def solution(mesh):
    rows, cols, reps = (mesh.shape[axis] for axis in ("row", "col", "rep"))

    def body(density, keep_square, keep_cube):
        tile, wide = density.shape
        if cols == 2 and rows == 2 * cols and reps == 4 and tile * rows == wide * cols:
            return by_whole(reps, density, keep_square, keep_cube)
        return by_panel(rows, cols, reps, tile * rows, density, keep_square, keep_cube)

    return jax.shard_map(
        body,
        mesh=mesh,
        in_specs=(P("row", "col"), P("row", "col"), P("row", "col")),
        out_specs=P(("row", "rep"), "col"),
        check_vma=False,
    )
```

```python
import functools

import jax
import jax.numpy as jnp
from jax import lax
from jax.experimental import pallas as pl
from jax.experimental.pallas import tpu as pltpu
from jax.sharding import PartitionSpec as P

MESH = pl.DeviceIdType.MESH

def flip(index, bit):
    return index + bit - 2 * bit * (index // bit % 2)


def panel_kernel(rows, cols, reps, block, chunks, density, keep_square, keep_cube, out,
           panel, left, low, total, z_send, z_recv, r_send, r_recv, a_send, a_recv,
           l_send, l_recv, local_sem):
    tile_rows, tile_cols = density.shape
    own = tile_rows // reps
    piece = own // chunks
    ratio = tile_cols // tile_rows
    z, c, p = lax.axis_index("row"), lax.axis_index("col"), lax.axis_index("rep")
    bits = []
    bit = reps // 2
    while bit:
        bits.append(bit)
        bit //= 2
    others = [lax.rem(c + step, cols) for step in range(1, cols)]

    barrier = pltpu.get_barrier_semaphore()
    for step, ok in ((1, z < rows - 1), (-1, z > 0)):
        @pl.when(ok)
        def _():
            pl.semaphore_signal(barrier, inc=1, device_id={"row": z + step}, device_id_type=MESH)
    for bit in bits:
        pl.semaphore_signal(barrier, inc=1, device_id={"rep": flip(p, bit)}, device_id_type=MESH)
    for other in others:
        pl.semaphore_signal(barrier, inc=1, device_id={"col": other}, device_id_type=MESH)
    keep_tile = pltpu.make_async_copy(
        density, panel.at[pl.ds(pl.multiple_of(z * tile_rows, tile_rows), tile_rows)], local_sem.at[0])
    keep_tile.start()
    keep_left = [
        pltpu.make_async_copy(
            density.at[pl.ds(pl.multiple_of(p * own, own), own), pl.ds(part * tile_rows, tile_rows)],
            left.at[c * ratio + part], local_sem.at[1 + part])
        for part in range(ratio)
    ]
    for copy in keep_left:
        copy.start()
    below, above = (z + rows - 1) // rows, (2 * rows - 2 - z) // rows
    pl.semaphore_wait(barrier, len(bits) + len(others) + below + above)

    def slot(t, member, q):
        return panel.at[pl.ds(pl.multiple_of(t * tile_rows + member * own + q * piece, piece), piece)]

    def packed(t, place):
        return t - (t - place - 1 + rows) // rows

    def z_copy(t, q, step, first=False, sending=True):
        at = z if sending else z - step
        source = slot(t, p, q)
        if first:
            source = density.at[pl.ds(pl.multiple_of(p * own + q * piece, piece), piece)]
        return pltpu.make_async_remote_copy(
            source, slot(t, p, q), z_send.at[t + (1 - step) // 2, q],
            z_recv.at[packed(t, at + step), q],
            device_id={"row": z + step}, device_id_type=MESH)

    def r_copies(t, q, stage):
        members = [p]
        for bit in bits[:stage]:
            members = members + [flip(member, bit) for member in members]
        peer = flip(p, bits[stage])
        base = 2 ** stage - 1
        return [
            pltpu.make_async_remote_copy(
                slot(t, member, q), slot(t, member, q), r_send.at[base + i, packed(t, z), q],
                r_recv.at[base + i, packed(t, z), q], device_id={"rep": peer}, device_id_type=MESH)
            for i, member in enumerate(members)
        ]

    def r_waits(t, q, stage):
        peer = flip(p, bits[stage])
        members = [peer]
        for bit in bits[:stage]:
            members = members + [flip(member, bit) for member in members]
        base = 2 ** stage - 1
        for i, member in enumerate(members):
            pltpu.make_async_remote_copy(
                slot(t, member, q), slot(t, member, q), r_send.at[base + i, packed(t, z), q],
                r_recv.at[base + i, packed(t, z), q], device_id={"rep": peer}, device_id_type=MESH).wait_recv()

    def a_copy(owner, peer, part):
        return pltpu.make_async_remote_copy(
            density.at[pl.ds(pl.multiple_of(p * own, own), own), pl.ds(part * tile_rows, tile_rows)],
            left.at[owner * ratio + part], a_send.at[peer, part], a_recv.at[owner, part],
            device_id={"col": peer}, device_id_type=MESH)

    def l_copy(owner, peer, part):
        return pltpu.make_async_remote_copy(
            low.at[owner * ratio + part], low.at[owner * ratio + part],
            l_send.at[peer, part], l_recv.at[owner, part],
            device_id={"col": peer}, device_id_type=MESH)

    ways = ((1, z < rows - 1), (-1, z > 0))
    for q in range(chunks):
        for step, ok in ways:
            @pl.when(ok)
            def _():
                z_copy(z, q, step, True).start()
    for other in others:
        for part in range(ratio):
            a_copy(c, other, part).start()

    def arrivals(distance):
        return ((1, z - distance, z - distance >= 0, z < rows - 1),
                (-1, z + distance, z + distance < rows, z > 0))

    def take(distance):
        for q in range(chunks):
            for step, t, ok, onward in arrivals(distance):
                @pl.when(ok)
                def _():
                    z_copy(t, q, step, sending=False).wait_recv()

                    @pl.when(onward)
                    def _():
                        z_copy(t, q, step).start()
                    for copy in r_copies(t, q, 0):
                        copy.start()

    def spread(distance, stage):
        for q in range(chunks):
            for step, t, ok, onward in arrivals(distance):
                @pl.when(ok)
                def _():
                    r_waits(t, q, stage - 1)
                    for copy in r_copies(t, q, stage):
                        copy.start()

    def product(factor, t):
        return jnp.dot(factor[t], panel[pl.ds(pl.multiple_of(t * tile_rows, tile_rows), tile_rows), :],
                       preferred_element_type=jnp.float32)

    def use(distance):
        for step, t, ok, onward in arrivals(distance):
            @pl.when(ok)
            def _():
                for q in range(chunks):
                    r_waits(t, q, len(bits) - 1)
                total[...] += product(left, t)

    keep_tile.wait()
    for copy in keep_left:
        copy.wait()
    started = False
    for distance in range(1, rows + len(bits)):
        if distance < rows:
            take(distance)
        for stage in range(1, len(bits)):
            if 1 <= distance - stage < rows:
                spread(distance - stage, stage)
        if not started:
            for other in others:
                for part in range(ratio):
                    a_copy(other, other, part).wait_recv()
            total[...] = product(left, z)
            started = True
        if 1 <= distance - len(bits) < rows:
            use(distance - len(bits))

    row_block = (p * own + lax.broadcasted_iota(jnp.int32, (own, block), 0)) // block

    def widen(keep, column):
        wide = jnp.zeros((own, block), jnp.float32)
        for i in range(tile_rows // block):
            wide = jnp.where(row_block == i, keep[i, column].astype(jnp.float32), wide)
        return wide

    per_part = tile_rows // block
    for column in range(tile_cols // block):
        span = pl.ds(column * block, block)
        square = total[:, span] * widen(keep_square, column)
        total[:, span] = square
        low[c * ratio + column // per_part, :, pl.ds(column % per_part * block, block)] = square.astype(jnp.bfloat16)
    for other in others:
        for part in range(ratio):
            l_copy(c, other, part).start()
    cube = product(low, c * ratio)
    for part in range(1, ratio):
        cube = cube + product(low, c * ratio + part)
    out[...] = cube
    for other in others:
        for part in range(ratio):
            l_copy(other, other, part).wait_recv()
            out[...] += product(low, other * ratio + part)
    for column in range(tile_cols // block):
        span = pl.ds(column * block, block)
        out[:, span] = 3.0 * total[:, span] - 2.0 * (out[:, span] * widen(keep_cube, column))

    for q in range(chunks):
        for step, ok in ways:
            @pl.when(ok)
            def _():
                z_copy(z, q, step, True).wait_send()
        for distance in range(1, rows):
            for step, t, ok, onward in arrivals(distance):
                @pl.when(ok)
                def _():
                    @pl.when(onward)
                    def _():
                        z_copy(t, q, step).wait_send()
                    for stage in range(len(bits)):
                        for copy in r_copies(t, q, stage):
                            copy.wait_send()
    for other in others:
        for part in range(ratio):
            a_copy(c, other, part).wait_send()
            l_copy(c, other, part).wait_send()


def by_panel(rows, cols, reps, mat, density, keep_square, keep_cube):
    tile_rows, tile_cols = density.shape
    block = tile_rows // keep_square.shape[0]
    own = tile_rows // reps
    ratio = tile_cols // tile_rows
    chunks = 3 if own % 48 == 0 else 1
    dma = pltpu.SemaphoreType.DMA
    return pl.pallas_call(
        functools.partial(panel_kernel, rows, cols, reps, block, chunks),
        out_shape=pltpu.VMEM((own, tile_cols), jnp.float32),
        in_specs=[
            pl.BlockSpec(memory_space=pl.ANY),
            pl.BlockSpec(memory_space=pltpu.SMEM),
            pl.BlockSpec(memory_space=pltpu.SMEM),
        ],
        out_specs=pl.BlockSpec(memory_space=pltpu.VMEM),
        scratch_shapes=[
            pltpu.VMEM((mat, tile_cols), jnp.bfloat16),
            pltpu.VMEM((rows, own, tile_rows), jnp.bfloat16),
            pltpu.VMEM((rows, own, tile_rows), jnp.bfloat16),
            pltpu.VMEM((own, tile_cols), jnp.float32),
            dma((rows + 1, chunks)),
            dma((rows - 1, chunks)),
            dma((reps - 1, rows - 1, chunks)),
            dma((reps - 1, rows - 1, chunks)),
            dma((cols, ratio)),
            dma((cols, ratio)),
            dma((cols, ratio)),
            dma((cols, ratio)),
            dma((1 + ratio,)),
        ],
        compiler_params=pltpu.CompilerParams(collective_id=0, has_side_effects=True),
    )(density, keep_square, keep_cube)


ARRIVALS = {"x_keep": 1, "x_own": 4, "y_own": 3, "z_diag": 1, "z_off": 4, "y_off": 1, "c_part": 4, "x_part": 4,
            "y_part": 4, "v_part": 4, "t_far": 1, "t_diag": 1, "t_off": 1, "t_part": 1}
SENDS = {"x_keep": 0, "x_own": 1, "y_own": 1, "z_diag": 2, "z_off": 2, "y_off": 2, "c_part": 3, "x_part": 3,
         "y_part": 3, "v_part": 3, "t_far": 4, "t_off": 4, "t_diag": 5, "t_part": 5}


def whole_kernel(reps, block, density, keep_square, keep_cube_in, out,
                 tiles, cross, corner, keeps, keep_cube, square, low, keep_wide, local_sem, ready, sends, *sems):
    arrivals = dict(zip(ARRIVALS, sems))
    tile, wide = density.shape
    own = tile // reps
    strips = tile // block
    sub = block // reps
    every = range(strips)
    z, c, p = lax.axis_index("row"), lax.axis_index("col"), lax.axis_index("rep")
    half, here = z // 2, z % 2
    there, other, far = 1 - here, 1 - half, 1 - c
    across = p + reps // 2 - reps * (p // (reps // 2))
    twin = p + 1 - 2 * (p % 2)
    is_diag, is_inner = c == half, here != half
    to_far, to_mate = {"col": far}, {"row": z + 1 - 2 * here}
    to_across, to_twin, to_corner = {"rep": across}, {"rep": twin}, {"col": far, "rep": across}
    quarters = (p, across)
    twins = (twin, across + 1 - 2 * (across % 2))
    distant = (3 * other, other + 1)
    near, end = 1 - other, other
    from_far, from_diag = (0, 2), (1, 3)

    def remote(source, target, name, index, device):
        return pltpu.make_async_remote_copy(
            source, target, sends.at[SENDS[name]], arrivals[name].at[index], device_id=device, device_id_type=MESH)

    def bulk(width):
        blocks = width * sub // block
        many = next(m for m in range(wide // block, 0, -1)
                    if blocks % (16 * m) == 0 and blocks // m <= tile)
        return cross.at[pl.ds(0, blocks // many), pl.ds(0, many * block)]

    def arrived(name, index, width):
        ref = bulk(width)
        remote(ref, ref, name, index, to_mate).wait_recv()

    def sent(name, width):
        ref = bulk(width)
        remote(ref, ref, name, 0, to_mate).wait_send()

    def rows(q, s):
        return pl.ds(pl.multiple_of(s * block + q * sub, sub), sub)

    def columns(start, size):
        return pl.ds(pl.multiple_of(start, block), size)

    def level_at(level):
        return columns(level * tile, tile)

    def relay(ref, name, index, device):
        return remote(ref, ref, name, index, device)

    def own_out(name, j, s, device):
        at = rows(quarters[j], s)
        index = s if j == 0 else strips
        return remote(density.at[at], tiles.at[c, here, at], name, index, device)

    def tile_at(column, level, q, s):
        return tiles.at[column, level, rows(q, s)]

    def diag_at(level, q, s):
        return tiles.at[half, level, rows(q, s), columns(level * tile + s * block, tile - s * block)]

    def part_at(i, q, of=other, source=False):
        if i < strips:
            band = of * i + (1 - of) * (strips - 1 - i)
            ref = density if source else cross
            return [ref.at[rows(q, band), columns(of * i * block, wide - i * block)]]
        if source:
            return [density.at[rows(q, s), columns(here * tile + s * block, tile - s * block)] for s in every]
        return [corner.at[rows(q, s), columns(s * block, tile - s * block)] for s in every]

    triangle = sum(tile - s * block for s in every)
    part_width = [wide - s * block for s in every] + [triangle]

    def part_out(i, d, column):
        for source, target in zip(part_at(i, p, half, True), part_at(i, p, half)):
            remote(source, target, "c_part", i, {"row": distant[d], "col": column}).start()

    def part_on(name, i, q, device, index=None):
        for ref in part_at(i, q):
            relay(ref, name, i if index is None else index, device).start()

    def twin_part(j, i):
        part_on("t_part", i, quarters[j], to_twin, 0)

    def twin_tile(name, column, level, j, s):
        relay(tile_at(column, level, quarters[j], s), name, 0, to_twin).start()

    def twin_diag(j):
        for s in every:
            relay(diag_at(there, quarters[j], s), "t_diag", 0, to_twin).start()

    def keep_copy(at):
        return remote(keep_square, keeps.at[at], "x_keep", 0, to_far)

    def spread(i):
        arrived("c_part", i, part_width[i])
        part_on("v_part", i, p, to_corner)
        part_on("y_part", i, p, to_across)
        part_on("x_part", i, p, to_far)
        twin_part(0, i)

    def gather(mine, theirs):
        for i in theirs:
            arrived("x_part", i, part_width[i])
            twin_part(0, i)
        for i in mine:
            arrived("y_part", i, part_width[i])
            twin_part(1, i)
        for i in theirs:
            arrived("v_part", i, part_width[i])
            twin_part(1, i)

    barrier = pltpu.get_barrier_semaphore()
    beside = (to_far, to_mate, to_across, to_twin)
    for device in beside:
        pl.semaphore_signal(barrier, inc=1, device_id=device, device_id_type=MESH)
    is_low = half == 0

    @pl.when(is_low)
    def _():
        for at in distant:
            pl.semaphore_signal(barrier, inc=1, device_id={"row": at, "col": other}, device_id_type=MESH)

    @pl.when(is_low & is_diag)
    def _():
        for column in (c, far):
            pl.semaphore_signal(barrier, inc=1, device_id={"row": distant[1], "col": column}, device_id_type=MESH)

    tile_copy = pltpu.make_async_copy(density, tiles.at[c, here], local_sem.at[0])
    tile_copy.start()
    keep_local = pltpu.make_async_copy(keep_square, keeps.at[c], local_sem.at[1])
    keep_local.start()
    keep_cube_copy = pltpu.make_async_copy(keep_cube_in, keep_cube, local_sem.at[2])
    keep_cube_copy.start()

    row_block = (p * own + lax.broadcasted_iota(jnp.int32, (own, block), 0)) // block

    def widen(at, keep, scale):
        for column in range(wide // block):
            value = jnp.zeros((own, block), jnp.float32)
            for i in range(tile // block):
                value = jnp.where(row_block == i, keep(i, column).astype(jnp.float32) * scale, value)
            keep_wide[at, :, pl.ds(column * block, block)] = value

    def parts_out():
        for d in range(2):
            @pl.when(is_inner)
            def _():
                for i in (1, 0, 2):
                    part_out(i, d, far if i in from_diag else c)

            @pl.when(jnp.logical_not(is_inner))
            def _():
                part_out(strips, d, far)

    @pl.when(is_low)
    def _():
        pl.semaphore_wait(barrier, len(beside))

    @pl.when(jnp.logical_not(is_low))
    def _():
        for diag, inner in ((1, 1), (1, 0), (0, 1), (0, 0)):
            @pl.when((is_diag.astype(jnp.int32) == diag) & (is_inner.astype(jnp.int32) == inner))
            def _():
                pl.semaphore_wait(barrier, len(beside) + 4 * diag + 2 * inner)

        @pl.when(is_inner)
        def _():
            for at in distant:
                pl.semaphore_signal(ready, inc=1, device_id={"row": at, "col": other}, device_id_type=MESH)

        @pl.when(is_diag)
        def _():
            parts_out()

    keep_copy(c).start()
    for s in every:
        own_out("x_own", 0, s, to_far).start()

    @pl.when(is_diag)
    def _():
        for s in every:
            own_out("x_own", 1, s, to_far).start()
        for j in range(2):
            for s in every:
                remote(density.at[rows(quarters[j], s), columns(here * tile + s * block, tile - s * block)],
                       diag_at(here, quarters[j], s), "z_diag", 0, to_mate).start()

        for s in every:
            arrived("x_own", s, wide)
            if s == 0:
                @pl.when(is_low)
                def _():
                    pl.semaphore_wait(ready, 2)
                    parts_out()
            relay(tile_at(other, here, p, s), "y_own", s, to_across).start()
            relay(tile_at(other, here, p, s), "z_off", s, to_mate).start()
            twin_tile("t_far", other, here, 0, s)
        arrived("z_diag", 0, 2 * triangle)
        for j in range(2):
            twin_diag(j)
        @pl.when(jnp.logical_not(is_inner))
        def _():
            spread(1)
        for s in every:
            arrived("y_own", s, wide)
            relay(tile_at(other, here, across, s), "z_off", strips, to_mate).start()
            twin_tile("t_far", other, here, 1, s)
        @pl.when(is_inner)
        def _():
            spread(1)
        spread(strips)
        for s in every:
            arrived("z_off", s, wide)
            twin_tile("t_off", other, there, 0, s)

    @pl.when(jnp.logical_not(is_diag))
    def _():
        for s in every:
            own_out("z_off", 0, s, to_mate).start()
        for s in every:
            arrived("z_off", s, wide)
            relay(tile_at(other, there, p, s), "y_off", 0, to_across).start()
            twin_tile("t_off", other, there, 0, s)

        def pass_far(j, s):
            relay(diag_at(here, quarters[j], s), "z_diag", 0, to_mate).start()
            twin_tile("t_far", half, here, j, s)

        for s in every:
            arrived("x_own", s, wide)
            pass_far(0, s)
        for i in from_far:
            spread(i)
        arrived("x_own", strips, strips * wide)
        for s in every:
            pass_far(1, s)
        arrived("y_off", 0, strips * wide)
        for s in every:
            twin_tile("t_off", other, there, 1, s)
        arrived("z_diag", 0, 2 * triangle)
        for j in range(2):
            twin_diag(j)

    tile_copy.wait()
    keep_cube_copy.wait()
    widen(2, lambda i, j: keep_cube[i, j], -2.0)
    keep_local.wait()
    widen(c, lambda i, j: keeps[c, i, j], 1.0)
    keep_copy(far).wait_recv()
    widen(far, lambda i, j: keeps[far, i, j], 1.0)

    def dot(a, b, contract=0):
        return lax.dot_general(a, b, (((1,), (contract,)), ((), ())), preferred_element_type=jnp.float32)

    def complete(ref, lead, level, source_first):
        for a in every:
            for b in range(a + 1, strips):
                r, t = (a, b) if source_first is None else (b + source_first * (a - b), a + source_first * (b - a))
                block_at = lambda i, j: lead + (columns(i * block, block), columns(level * tile + j * block, block))
                ref[block_at(t, r)] = ref[block_at(r, t)].T

    def by_diag(left_here, left_there):
        a = tiles[half, here, :, level_at(here)]
        b = tiles[half, here, :, level_at(there)]
        d = tiles[half, there, :, level_at(there)]
        return dot(left_here, a) + dot(left_there, b, 1), dot(left_here, b) + dot(left_there, d)

    def by_cross(left_near, left_end):
        a = cross[:, level_at(near)]
        b = cross[:, level_at(end)]
        return dot(left_near, a) + dot(left_end, b, 1), dot(left_near, b) + dot(left_end, corner[...])

    my_rows = pl.ds(pl.multiple_of(p * own, own), own)

    arrived("t_diag", 0, 2 * triangle)
    arrived("t_far", 0, 2 * strips * wide)
    complete(tiles, (half, there), there, None)
    lh = [tiles[half, here, my_rows, level_at(level)] for level in (here, there)]
    lo = tiles[other, here, my_rows, :]
    h_here, h_there = by_diag(*lh)
    square[half, :, level_at(here)] = h_here + dot(lo, tiles[other, here], 1)
    square[half, :, level_at(there)] = h_there
    square[other] = dot(lh[0], tiles[other, here])

    @pl.when(is_diag)
    def _():
        arrived("z_off", strips, strips * wide)
        for s in every:
            twin_tile("t_off", other, there, 1, s)
        gather(from_diag, from_far)

    @pl.when(jnp.logical_not(is_diag))
    def _():
        gather(from_far, from_diag)

    arrived("t_off", 0, 2 * strips * wide)

    def mask(at):
        value = square[at] * keep_wide[at]
        square[at] = value
        low[at] = value.astype(jnp.bfloat16)

    square[half, :, level_at(there)] += dot(lo, tiles[other, there], 1)
    mask(half)
    square[other] += dot(lh[1], tiles[other, there])

    @pl.when(is_diag)
    def _():
        h_here, h_there = by_diag(low[half, :, level_at(here)], low[half, :, level_at(there)])
        out[:, level_at(here)] = h_here
        out[:, level_at(there)] = h_there

    @pl.when(jnp.logical_not(is_diag))
    def _():
        out[...] = (dot(low[half, :, level_at(here)], tiles[other, here])
                    + dot(low[half, :, level_at(there)], tiles[other, there]))

    arrived("t_part", 0, 2 * sum(part_width))
    complete(cross, (), near, other)
    complete(corner, (), 0, None)
    o_near, o_end = by_cross(*(tiles[other, here, my_rows, level_at(level)] for level in (near, end)))
    square[other, :, level_at(near)] += o_near
    square[other, :, level_at(end)] += o_end
    mask(other)

    @pl.when(is_diag)
    def _():
        for level in (here, there):
            span = level_at(level)
            cube = out[:, span] + dot(low[other], tiles[other, level], 1)
            out[:, span] = 3.0 * square[c, :, span] + cube * keep_wide[2, :, span]

    @pl.when(jnp.logical_not(is_diag))
    def _():
        cubes = by_cross(low[other, :, level_at(near)], low[other, :, level_at(end)])
        for level, part in zip((near, end), cubes):
            span = level_at(level)
            cube = out[:, span] + part
            out[:, span] = 3.0 * square[c, :, span] + cube * keep_wide[2, :, span]

    keep_copy(c).wait_send()
    sent("t_off", 4 * strips * wide)
    sent("t_part", 2 * triangle + 2 * sum(part_width))

    @pl.when(is_diag)
    def _():
        sent("x_own", 3 * strips * wide)
        sent("z_off", 2 * strips * wide + 2 * triangle)
        onward = 3 * sum(part_width[i] for i in from_diag)

        @pl.when(is_inner)
        def _():
            sent("c_part", onward + 2 * sum(part_width[:strips]))

        @pl.when(jnp.logical_not(is_inner))
        def _():
            sent("c_part", onward + 2 * triangle)

    @pl.when(jnp.logical_not(is_diag))
    def _():
        sent("x_own", strips * wide)
        sent("z_off", 2 * strips * wide + 2 * triangle)
        sent("c_part", 3 * sum(part_width[i] for i in from_far))


def by_whole(reps, density, keep_square, keep_cube):
    tile, wide = density.shape
    block = tile // keep_square.shape[0]
    own = tile // reps
    strips = tile // block
    dma = pltpu.SemaphoreType.DMA
    low = jnp.bfloat16
    return pl.pallas_call(
        functools.partial(whole_kernel, reps, block),
        out_shape=pltpu.VMEM((own, wide), jnp.float32),
        in_specs=[
            pl.BlockSpec(memory_space=pl.ANY),
            pl.BlockSpec(memory_space=pl.ANY),
            pl.BlockSpec(memory_space=pl.ANY),
        ],
        out_specs=pl.BlockSpec(memory_space=pltpu.VMEM),
        scratch_shapes=[
            pltpu.VMEM((2, 2, tile, wide), low),
            pltpu.VMEM((tile, wide), low),
            pltpu.VMEM((tile, tile), low),
            pltpu.SMEM((2,) + keep_square.shape, jnp.int32),
            pltpu.SMEM(keep_cube.shape, jnp.int32),
            pltpu.VMEM((2, own, wide), jnp.float32),
            pltpu.VMEM((2, own, wide), low),
            pltpu.VMEM((3, own, wide), jnp.float32),
            dma((3,)),
            pltpu.SemaphoreType.REGULAR,
            dma((max(SENDS.values()) + 1,)),
        ] + [dma((count,)) for count in ARRIVALS.values()],
        compiler_params=pltpu.CompilerParams(collective_id=0, has_side_effects=True),
    )(density, keep_square, keep_cube)


def solution(mesh):
    rows, cols, reps = (mesh.shape[axis] for axis in ("row", "col", "rep"))

    def body(density, keep_square, keep_cube):
        tile, wide = density.shape
        if cols == 2 and rows == 2 * cols and reps == 4 and tile * rows == wide * cols:
            return by_whole(reps, density, keep_square, keep_cube)
        return by_panel(rows, cols, reps, tile * rows, density, keep_square, keep_cube)

    return jax.shard_map(
        body,
        mesh=mesh,
        in_specs=(P("row", "col"), P("row", "col"), P("row", "col")),
        out_specs=P(("row", "rep"), "col"),
        check_vma=False,
    )
```

```python
import functools

import jax
import jax.numpy as jnp
from jax import lax
from jax.experimental import pallas as pl
from jax.experimental.pallas import tpu as pltpu
from jax.sharding import PartitionSpec as P

MESH = pl.DeviceIdType.MESH

def flip(index, bit):
    return index + bit - 2 * bit * (index // bit % 2)


def panel_kernel(rows, cols, reps, block, chunks, density, keep_square, keep_cube, out,
           panel, left, low, total, z_send, z_recv, r_send, r_recv, a_send, a_recv,
           l_send, l_recv, local_sem):
    tile_rows, tile_cols = density.shape
    own = tile_rows // reps
    piece = own // chunks
    ratio = tile_cols // tile_rows
    z, c, p = lax.axis_index("row"), lax.axis_index("col"), lax.axis_index("rep")
    bits = []
    bit = reps // 2
    while bit:
        bits.append(bit)
        bit //= 2
    others = [lax.rem(c + step, cols) for step in range(1, cols)]

    barrier = pltpu.get_barrier_semaphore()
    for step, ok in ((1, z < rows - 1), (-1, z > 0)):
        @pl.when(ok)
        def _():
            pl.semaphore_signal(barrier, inc=1, device_id={"row": z + step}, device_id_type=MESH)
    for bit in bits:
        pl.semaphore_signal(barrier, inc=1, device_id={"rep": flip(p, bit)}, device_id_type=MESH)
    for other in others:
        pl.semaphore_signal(barrier, inc=1, device_id={"col": other}, device_id_type=MESH)
    keep_tile = pltpu.make_async_copy(
        density, panel.at[pl.ds(pl.multiple_of(z * tile_rows, tile_rows), tile_rows)], local_sem.at[0])
    keep_tile.start()
    keep_left = [
        pltpu.make_async_copy(
            density.at[pl.ds(pl.multiple_of(p * own, own), own), pl.ds(part * tile_rows, tile_rows)],
            left.at[c * ratio + part], local_sem.at[1 + part])
        for part in range(ratio)
    ]
    for copy in keep_left:
        copy.start()
    below, above = (z + rows - 1) // rows, (2 * rows - 2 - z) // rows
    pl.semaphore_wait(barrier, len(bits) + len(others) + below + above)

    def slot(t, member, q):
        return panel.at[pl.ds(pl.multiple_of(t * tile_rows + member * own + q * piece, piece), piece)]

    def packed(t, place):
        return t - (t - place - 1 + rows) // rows

    def z_copy(t, q, step, first=False, sending=True):
        at = z if sending else z - step
        source = slot(t, p, q)
        if first:
            source = density.at[pl.ds(pl.multiple_of(p * own + q * piece, piece), piece)]
        return pltpu.make_async_remote_copy(
            source, slot(t, p, q), z_send.at[t + (1 - step) // 2, q],
            z_recv.at[packed(t, at + step), q],
            device_id={"row": z + step}, device_id_type=MESH)

    def r_copies(t, q, stage):
        members = [p]
        for bit in bits[:stage]:
            members = members + [flip(member, bit) for member in members]
        peer = flip(p, bits[stage])
        base = 2 ** stage - 1
        return [
            pltpu.make_async_remote_copy(
                slot(t, member, q), slot(t, member, q), r_send.at[base + i, packed(t, z), q],
                r_recv.at[base + i, packed(t, z), q], device_id={"rep": peer}, device_id_type=MESH)
            for i, member in enumerate(members)
        ]

    def r_waits(t, q, stage):
        peer = flip(p, bits[stage])
        members = [peer]
        for bit in bits[:stage]:
            members = members + [flip(member, bit) for member in members]
        base = 2 ** stage - 1
        for i, member in enumerate(members):
            pltpu.make_async_remote_copy(
                slot(t, member, q), slot(t, member, q), r_send.at[base + i, packed(t, z), q],
                r_recv.at[base + i, packed(t, z), q], device_id={"rep": peer}, device_id_type=MESH).wait_recv()

    def a_copy(owner, peer, part):
        return pltpu.make_async_remote_copy(
            density.at[pl.ds(pl.multiple_of(p * own, own), own), pl.ds(part * tile_rows, tile_rows)],
            left.at[owner * ratio + part], a_send.at[peer, part], a_recv.at[owner, part],
            device_id={"col": peer}, device_id_type=MESH)

    def l_copy(owner, peer, part):
        return pltpu.make_async_remote_copy(
            low.at[owner * ratio + part], low.at[owner * ratio + part],
            l_send.at[peer, part], l_recv.at[owner, part],
            device_id={"col": peer}, device_id_type=MESH)

    ways = ((1, z < rows - 1), (-1, z > 0))
    for q in range(chunks):
        for step, ok in ways:
            @pl.when(ok)
            def _():
                z_copy(z, q, step, True).start()
    for other in others:
        for part in range(ratio):
            a_copy(c, other, part).start()

    def arrivals(distance):
        return ((1, z - distance, z - distance >= 0, z < rows - 1),
                (-1, z + distance, z + distance < rows, z > 0))

    def take(distance):
        for q in range(chunks):
            for step, t, ok, onward in arrivals(distance):
                @pl.when(ok)
                def _():
                    z_copy(t, q, step, sending=False).wait_recv()

                    @pl.when(onward)
                    def _():
                        z_copy(t, q, step).start()
                    for copy in r_copies(t, q, 0):
                        copy.start()

    def spread(distance, stage):
        for q in range(chunks):
            for step, t, ok, onward in arrivals(distance):
                @pl.when(ok)
                def _():
                    r_waits(t, q, stage - 1)
                    for copy in r_copies(t, q, stage):
                        copy.start()

    def product(factor, t):
        return jnp.dot(factor[t], panel[pl.ds(pl.multiple_of(t * tile_rows, tile_rows), tile_rows), :],
                       preferred_element_type=jnp.float32)

    def use(distance):
        for step, t, ok, onward in arrivals(distance):
            @pl.when(ok)
            def _():
                for q in range(chunks):
                    r_waits(t, q, len(bits) - 1)
                total[...] += product(left, t)

    keep_tile.wait()
    for copy in keep_left:
        copy.wait()
    started = False
    for distance in range(1, rows + len(bits)):
        if distance < rows:
            take(distance)
        for stage in range(1, len(bits)):
            if 1 <= distance - stage < rows:
                spread(distance - stage, stage)
        if not started:
            for other in others:
                for part in range(ratio):
                    a_copy(other, other, part).wait_recv()
            total[...] = product(left, z)
            started = True
        if 1 <= distance - len(bits) < rows:
            use(distance - len(bits))

    row_block = (p * own + lax.broadcasted_iota(jnp.int32, (own, block), 0)) // block

    def widen(keep, column):
        wide = jnp.zeros((own, block), jnp.float32)
        for i in range(tile_rows // block):
            wide = jnp.where(row_block == i, keep[i, column].astype(jnp.float32), wide)
        return wide

    per_part = tile_rows // block
    for column in range(tile_cols // block):
        span = pl.ds(column * block, block)
        square = total[:, span] * widen(keep_square, column)
        total[:, span] = square
        low[c * ratio + column // per_part, :, pl.ds(column % per_part * block, block)] = square.astype(jnp.bfloat16)
    for other in others:
        for part in range(ratio):
            l_copy(c, other, part).start()
    cube = product(low, c * ratio)
    for part in range(1, ratio):
        cube = cube + product(low, c * ratio + part)
    out[...] = cube
    for other in others:
        for part in range(ratio):
            l_copy(other, other, part).wait_recv()
            out[...] += product(low, other * ratio + part)
    for column in range(tile_cols // block):
        span = pl.ds(column * block, block)
        out[:, span] = 3.0 * total[:, span] - 2.0 * (out[:, span] * widen(keep_cube, column))

    for q in range(chunks):
        for step, ok in ways:
            @pl.when(ok)
            def _():
                z_copy(z, q, step, True).wait_send()
        for distance in range(1, rows):
            for step, t, ok, onward in arrivals(distance):
                @pl.when(ok)
                def _():
                    @pl.when(onward)
                    def _():
                        z_copy(t, q, step).wait_send()
                    for stage in range(len(bits)):
                        for copy in r_copies(t, q, stage):
                            copy.wait_send()
    for other in others:
        for part in range(ratio):
            a_copy(c, other, part).wait_send()
            l_copy(c, other, part).wait_send()


def by_panel(rows, cols, reps, mat, density, keep_square, keep_cube):
    tile_rows, tile_cols = density.shape
    block = tile_rows // keep_square.shape[0]
    own = tile_rows // reps
    ratio = tile_cols // tile_rows
    chunks = 3 if own % 48 == 0 else 1
    dma = pltpu.SemaphoreType.DMA
    return pl.pallas_call(
        functools.partial(panel_kernel, rows, cols, reps, block, chunks),
        out_shape=pltpu.VMEM((own, tile_cols), jnp.float32),
        in_specs=[
            pl.BlockSpec(memory_space=pl.ANY),
            pl.BlockSpec(memory_space=pltpu.SMEM),
            pl.BlockSpec(memory_space=pltpu.SMEM),
        ],
        out_specs=pl.BlockSpec(memory_space=pltpu.VMEM),
        scratch_shapes=[
            pltpu.VMEM((mat, tile_cols), jnp.bfloat16),
            pltpu.VMEM((rows, own, tile_rows), jnp.bfloat16),
            pltpu.VMEM((rows, own, tile_rows), jnp.bfloat16),
            pltpu.VMEM((own, tile_cols), jnp.float32),
            dma((rows + 1, chunks)),
            dma((rows - 1, chunks)),
            dma((reps - 1, rows - 1, chunks)),
            dma((reps - 1, rows - 1, chunks)),
            dma((cols, ratio)),
            dma((cols, ratio)),
            dma((cols, ratio)),
            dma((cols, ratio)),
            dma((1 + ratio,)),
        ],
        compiler_params=pltpu.CompilerParams(collective_id=0, has_side_effects=True),
    )(density, keep_square, keep_cube)


ARRIVALS = {"x_keep": 1, "x_own": 4, "y_own": 3, "z_diag": 1, "z_off": 4, "y_off": 1, "c_part": 4, "x_part": 4,
            "y_part": 4, "v_part": 4, "t_far": 1, "t_diag": 1, "t_off": 1, "t_part": 1}
SENDS = {"x_keep": 0, "x_own": 1, "y_own": 1, "z_diag": 2, "z_off": 2, "y_off": 2, "c_part": 6, "x_part": 3,
         "y_part": 3, "v_part": 3, "t_far": 4, "t_off": 4, "t_diag": 5, "t_part": 5}


def whole_kernel(reps, block, density, keep_square, keep_cube_in, out,
                 tiles, cross, corner, keeps, keep_cube, square, low, keep_wide, local_sem, ready, sends, *sems):
    arrivals = dict(zip(ARRIVALS, sems))
    tile, wide = density.shape
    own = tile // reps
    strips = tile // block
    sub = block // reps
    every = range(strips)
    z, c, p = lax.axis_index("row"), lax.axis_index("col"), lax.axis_index("rep")
    half, here = z // 2, z % 2
    there, other, far = 1 - here, 1 - half, 1 - c
    across = p + reps // 2 - reps * (p // (reps // 2))
    twin = p + 1 - 2 * (p % 2)
    is_diag, is_inner = c == half, here != half
    to_far, to_mate = {"col": far}, {"row": z + 1 - 2 * here}
    to_across, to_twin, to_corner = {"rep": across}, {"rep": twin}, {"col": far, "rep": across}
    quarters = (p, across)
    twins = (twin, across + 1 - 2 * (across % 2))
    distant = (3 * other, other + 1)
    near, end = 1 - other, other
    from_far, from_diag = (0, 2), (1, 3)

    def remote(source, target, name, index, device):
        return pltpu.make_async_remote_copy(
            source, target, sends.at[SENDS[name]], arrivals[name].at[index], device_id=device, device_id_type=MESH)

    def bulk(width):
        blocks = width * sub // block
        many = next(m for m in range(wide // block, 0, -1)
                    if blocks % (16 * m) == 0 and blocks // m <= tile)
        return cross.at[pl.ds(0, blocks // many), pl.ds(0, many * block)]

    def arrived(name, index, width):
        ref = bulk(width)
        remote(ref, ref, name, index, to_mate).wait_recv()

    def sent(name, width):
        ref = bulk(width)
        remote(ref, ref, name, 0, to_mate).wait_send()

    def rows(q, s):
        return pl.ds(pl.multiple_of(s * block + q * sub, sub), sub)

    def columns(start, size):
        return pl.ds(pl.multiple_of(start, block), size)

    def level_at(level):
        return columns(level * tile, tile)

    def relay(ref, name, index, device):
        return remote(ref, ref, name, index, device)

    def own_out(name, j, s, device):
        at = rows(quarters[j], s)
        index = s if j == 0 else strips
        return remote(density.at[at], tiles.at[c, here, at], name, index, device)

    def tile_at(column, level, q, s):
        return tiles.at[column, level, rows(q, s)]

    def diag_at(level, q, s):
        return tiles.at[half, level, rows(q, s), columns(level * tile + s * block, tile - s * block)]

    def part_at(i, q, of=other, source=False):
        if i < strips:
            band = of * i + (1 - of) * (strips - 1 - i)
            ref = (density if i in from_far else tiles.at[half, here]) if source else cross
            return [ref.at[rows(q, band), columns(of * i * block, wide - i * block)]]
        if source:
            return [diag_at(here, q, s) for s in every]
        return [corner.at[rows(q, s), columns(s * block, tile - s * block)] for s in every]

    triangle = sum(tile - s * block for s in every)
    part_width = [wide - s * block for s in every] + [triangle]

    def part_out(i, d):
        for source, target in zip(part_at(i, p, half, True), part_at(i, p, half)):
            remote(source, target, "c_part", i, {"row": distant[d]}).start()

    def part_on(name, i, q, device, index=None):
        for ref in part_at(i, q):
            relay(ref, name, i if index is None else index, device).start()

    def twin_part(j, i):
        part_on("t_part", i, quarters[j], to_twin, 0)

    def twin_tile(name, column, level, j, s):
        relay(tile_at(column, level, quarters[j], s), name, 0, to_twin).start()

    def twin_diag(j):
        for s in every:
            relay(diag_at(there, quarters[j], s), "t_diag", 0, to_twin).start()

    def keep_copy(at):
        return remote(keep_square, keeps.at[at], "x_keep", 0, to_far)

    def spread(i):
        arrived("c_part", i, part_width[i])
        part_on("v_part", i, p, to_corner)
        part_on("y_part", i, p, to_across)
        part_on("x_part", i, p, to_far)
        twin_part(0, i)

    def gather(mine, theirs):
        for i in theirs:
            arrived("x_part", i, part_width[i])
            twin_part(0, i)
        for i in mine:
            arrived("y_part", i, part_width[i])
            twin_part(1, i)
        for i in theirs:
            arrived("v_part", i, part_width[i])
            twin_part(1, i)

    barrier = pltpu.get_barrier_semaphore()
    beside = (to_far, to_mate, to_across, to_twin)
    for device in beside:
        pl.semaphore_signal(barrier, inc=1, device_id=device, device_id_type=MESH)
    is_low = half == 0

    @pl.when(is_low)
    def _():
        for at in distant:
            pl.semaphore_signal(barrier, inc=1, device_id={"row": at}, device_id_type=MESH)

    tile_copy = pltpu.make_async_copy(density, tiles.at[c, here], local_sem.at[0])
    tile_copy.start()
    keep_local = pltpu.make_async_copy(keep_square, keeps.at[c], local_sem.at[1])
    keep_local.start()
    keep_cube_copy = pltpu.make_async_copy(keep_cube_in, keep_cube, local_sem.at[2])
    keep_cube_copy.start()

    row_block = (p * own + lax.broadcasted_iota(jnp.int32, (own, block), 0)) // block

    def widen(at, keep, scale):
        for column in range(wide // block):
            value = jnp.zeros((own, block), jnp.float32)
            for i in range(tile // block):
                value = jnp.where(row_block == i, keep(i, column).astype(jnp.float32) * scale, value)
            keep_wide[at, :, pl.ds(column * block, block)] = value

    def parts_out(parts):
        for d in range(2):
            for i in parts:
                part_out(i, d)

    def granted():
        @pl.when(is_low)
        def _():
            pl.semaphore_wait(ready, 1)

    @pl.when(is_low)
    def _():
        pl.semaphore_wait(barrier, len(beside))

    @pl.when(jnp.logical_not(is_low))
    def _():
        pl.semaphore_wait(barrier, len(beside) + 2)

        @pl.when(is_inner)
        def _():
            for at in distant:
                pl.semaphore_signal(ready, inc=1, device_id={"row": at}, device_id_type=MESH)

        @pl.when(is_diag & is_inner)
        def _():
            parts_out(from_far)

    keep_copy(c).start()
    first = (1, 0) + tuple(range(2, strips))
    for s in first:
        own_out("x_own", 0, s, to_far).start()

    @pl.when(is_diag)
    def _():
        for s in every:
            own_out("x_own", 1, s, to_far).start()
        for j in range(2):
            for s in every:
                remote(density.at[rows(quarters[j], s), columns(here * tile + s * block, tile - s * block)],
                       diag_at(here, quarters[j], s), "z_diag", 0, to_mate).start()

        for s in first:
            arrived("x_own", s, wide)
            if s == first[2]:
                granted()

                @pl.when(is_low & is_inner)
                def _():
                    parts_out(from_far)
            relay(tile_at(other, here, p, s), "y_own", s, to_across).start()
            relay(tile_at(other, here, p, s), "z_off", s, to_mate).start()
            twin_tile("t_far", other, here, 0, s)
        arrived("z_diag", 0, 2 * triangle)
        for j in range(2):
            twin_diag(j)
        @pl.when(jnp.logical_not(is_inner))
        def _():
            spread(1)
        for s in every:
            arrived("y_own", s, wide)
            relay(tile_at(other, here, across, s), "z_off", strips, to_mate).start()
            twin_tile("t_far", other, here, 1, s)
        @pl.when(is_inner)
        def _():
            spread(1)
        spread(strips)
        for s in every:
            arrived("z_off", s, wide)
            twin_tile("t_off", other, there, 0, s)

    @pl.when(jnp.logical_not(is_diag))
    def _():
        for s in every:
            own_out("z_off", 0, s, to_mate).start()
        for s in every:
            arrived("z_off", s, wide)
            relay(tile_at(other, there, p, s), "y_off", 0, to_across).start()
            twin_tile("t_off", other, there, 0, s)

        def pass_far(j, s):
            relay(diag_at(here, quarters[j], s), "z_diag", 0, to_mate).start()
            twin_tile("t_far", half, here, j, s)

        for s in first:
            arrived("x_own", s, wide)
            if s == first[0]:
                granted()

                @pl.when(is_inner)
                def _():
                    parts_out((1,))
            pass_far(0, s)

        @pl.when(jnp.logical_not(is_inner))
        def _():
            parts_out((strips,))
        for i in from_far:
            spread(i)
        arrived("x_own", strips, strips * wide)
        for s in every:
            pass_far(1, s)
        arrived("y_off", 0, strips * wide)
        for s in every:
            twin_tile("t_off", other, there, 1, s)
        arrived("z_diag", 0, 2 * triangle)
        for j in range(2):
            twin_diag(j)

    tile_copy.wait()
    keep_cube_copy.wait()
    widen(2, lambda i, j: keep_cube[i, j], -2.0)
    keep_local.wait()
    widen(c, lambda i, j: keeps[c, i, j], 1.0)
    keep_copy(far).wait_recv()
    widen(far, lambda i, j: keeps[far, i, j], 1.0)

    def dot(a, b, contract=0):
        return lax.dot_general(a, b, (((1,), (contract,)), ((), ())), preferred_element_type=jnp.float32)

    def complete(ref, lead, level, source_first):
        for a in every:
            for b in range(a + 1, strips):
                r, t = (a, b) if source_first is None else (b + source_first * (a - b), a + source_first * (b - a))
                block_at = lambda i, j: lead + (columns(i * block, block), columns(level * tile + j * block, block))
                ref[block_at(t, r)] = ref[block_at(r, t)].T

    def by_diag(left_here, left_there):
        a = tiles[half, here, :, level_at(here)]
        b = tiles[half, here, :, level_at(there)]
        d = tiles[half, there, :, level_at(there)]
        return dot(left_here, a) + dot(left_there, b, 1), dot(left_here, b) + dot(left_there, d)

    def by_cross(left_near, left_end):
        a = cross[:, level_at(near)]
        b = cross[:, level_at(end)]
        return dot(left_near, a) + dot(left_end, b, 1), dot(left_near, b) + dot(left_end, corner[...])

    my_rows = pl.ds(pl.multiple_of(p * own, own), own)

    arrived("t_diag", 0, 2 * triangle)
    arrived("t_far", 0, 2 * strips * wide)
    complete(tiles, (half, there), there, None)
    lh = [tiles[half, here, my_rows, level_at(level)] for level in (here, there)]
    lo = tiles[other, here, my_rows, :]
    h_here, h_there = by_diag(*lh)
    square[half, :, level_at(here)] = h_here + dot(lo, tiles[other, here], 1)
    square[half, :, level_at(there)] = h_there
    square[other] = dot(lh[0], tiles[other, here])

    @pl.when(is_diag)
    def _():
        arrived("z_off", strips, strips * wide)
        for s in every:
            twin_tile("t_off", other, there, 1, s)
        gather(from_diag, from_far)

    @pl.when(jnp.logical_not(is_diag))
    def _():
        gather(from_far, from_diag)

    arrived("t_off", 0, 2 * strips * wide)

    def mask(at):
        value = square[at] * keep_wide[at]
        square[at] = value
        low[at] = value.astype(jnp.bfloat16)

    square[half, :, level_at(there)] += dot(lo, tiles[other, there], 1)
    mask(half)
    square[other] += dot(lh[1], tiles[other, there])

    @pl.when(is_diag)
    def _():
        h_here, h_there = by_diag(low[half, :, level_at(here)], low[half, :, level_at(there)])
        out[:, level_at(here)] = h_here
        out[:, level_at(there)] = h_there

    @pl.when(jnp.logical_not(is_diag))
    def _():
        out[...] = (dot(low[half, :, level_at(here)], tiles[other, here])
                    + dot(low[half, :, level_at(there)], tiles[other, there]))

    arrived("t_part", 0, 2 * sum(part_width))
    complete(cross, (), near, other)
    complete(corner, (), 0, None)
    o_near, o_end = by_cross(*(tiles[other, here, my_rows, level_at(level)] for level in (near, end)))
    square[other, :, level_at(near)] += o_near
    square[other, :, level_at(end)] += o_end
    mask(other)

    @pl.when(is_diag)
    def _():
        for level in (here, there):
            span = level_at(level)
            cube = out[:, span] + dot(low[other], tiles[other, level], 1)
            out[:, span] = 3.0 * square[c, :, span] + cube * keep_wide[2, :, span]

    @pl.when(jnp.logical_not(is_diag))
    def _():
        cubes = by_cross(low[other, :, level_at(near)], low[other, :, level_at(end)])
        for level, part in zip((near, end), cubes):
            span = level_at(level)
            cube = out[:, span] + part
            out[:, span] = 3.0 * square[c, :, span] + cube * keep_wide[2, :, span]

    keep_copy(c).wait_send()
    sent("t_off", 4 * strips * wide)
    sent("t_part", 2 * triangle + 2 * sum(part_width))

    @pl.when(is_diag)
    def _():
        sent("x_own", 3 * strips * wide)
        sent("z_off", 2 * strips * wide + 2 * triangle)
        sent("x_part", 3 * sum(part_width[i] for i in from_diag))

        @pl.when(is_inner)
        def _():
            sent("c_part", 2 * sum(part_width[i] for i in from_far))

    @pl.when(jnp.logical_not(is_diag))
    def _():
        sent("x_own", strips * wide)
        sent("z_off", 2 * strips * wide + 2 * triangle)
        sent("x_part", 3 * sum(part_width[i] for i in from_far))

        @pl.when(is_inner)
        def _():
            sent("c_part", 2 * part_width[1])

        @pl.when(jnp.logical_not(is_inner))
        def _():
            sent("c_part", 2 * part_width[strips])


def by_whole(reps, density, keep_square, keep_cube):
    tile, wide = density.shape
    block = tile // keep_square.shape[0]
    own = tile // reps
    strips = tile // block
    dma = pltpu.SemaphoreType.DMA
    low = jnp.bfloat16
    return pl.pallas_call(
        functools.partial(whole_kernel, reps, block),
        out_shape=pltpu.VMEM((own, wide), jnp.float32),
        in_specs=[
            pl.BlockSpec(memory_space=pl.ANY),
            pl.BlockSpec(memory_space=pl.ANY),
            pl.BlockSpec(memory_space=pl.ANY),
        ],
        out_specs=pl.BlockSpec(memory_space=pltpu.VMEM),
        scratch_shapes=[
            pltpu.VMEM((2, 2, tile, wide), low),
            pltpu.VMEM((tile, wide), low),
            pltpu.VMEM((tile, tile), low),
            pltpu.SMEM((2,) + keep_square.shape, jnp.int32),
            pltpu.SMEM(keep_cube.shape, jnp.int32),
            pltpu.VMEM((2, own, wide), jnp.float32),
            pltpu.VMEM((2, own, wide), low),
            pltpu.VMEM((3, own, wide), jnp.float32),
            dma((3,)),
            pltpu.SemaphoreType.REGULAR,
            dma((max(SENDS.values()) + 1,)),
        ] + [dma((count,)) for count in ARRIVALS.values()],
        compiler_params=pltpu.CompilerParams(collective_id=0, has_side_effects=True),
    )(density, keep_square, keep_cube)


def solution(mesh):
    rows, cols, reps = (mesh.shape[axis] for axis in ("row", "col", "rep"))

    def body(density, keep_square, keep_cube):
        tile, wide = density.shape
        if cols == 2 and rows == 2 * cols and reps == 4 and tile * rows == wide * cols:
            return by_whole(reps, density, keep_square, keep_cube)
        return by_panel(rows, cols, reps, tile * rows, density, keep_square, keep_cube)

    return jax.shard_map(
        body,
        mesh=mesh,
        in_specs=(P("row", "col"), P("row", "col"), P("row", "col")),
        out_specs=P(("row", "rep"), "col"),
        check_vma=False,
    )
```

```python
import functools

import jax
import jax.numpy as jnp
from jax import lax
from jax.experimental import pallas as pl
from jax.experimental.pallas import tpu as pltpu
from jax.sharding import PartitionSpec as P

MESH = pl.DeviceIdType.MESH

def flip(index, bit):
    return index + bit - 2 * bit * (index // bit % 2)


def panel_kernel(rows, cols, reps, block, chunks, density, keep_square, keep_cube, out,
           panel, left, low, total, z_send, z_recv, r_send, r_recv, a_send, a_recv,
           l_send, l_recv, local_sem):
    tile_rows, tile_cols = density.shape
    own = tile_rows // reps
    piece = own // chunks
    ratio = tile_cols // tile_rows
    z, c, p = lax.axis_index("row"), lax.axis_index("col"), lax.axis_index("rep")
    bits = []
    bit = reps // 2
    while bit:
        bits.append(bit)
        bit //= 2
    others = [lax.rem(c + step, cols) for step in range(1, cols)]

    barrier = pltpu.get_barrier_semaphore()
    for step, ok in ((1, z < rows - 1), (-1, z > 0)):
        @pl.when(ok)
        def _():
            pl.semaphore_signal(barrier, inc=1, device_id={"row": z + step}, device_id_type=MESH)
    for bit in bits:
        pl.semaphore_signal(barrier, inc=1, device_id={"rep": flip(p, bit)}, device_id_type=MESH)
    for other in others:
        pl.semaphore_signal(barrier, inc=1, device_id={"col": other}, device_id_type=MESH)
    keep_tile = pltpu.make_async_copy(
        density, panel.at[pl.ds(pl.multiple_of(z * tile_rows, tile_rows), tile_rows)], local_sem.at[0])
    keep_tile.start()
    keep_left = [
        pltpu.make_async_copy(
            density.at[pl.ds(pl.multiple_of(p * own, own), own), pl.ds(part * tile_rows, tile_rows)],
            left.at[c * ratio + part], local_sem.at[1 + part])
        for part in range(ratio)
    ]
    for copy in keep_left:
        copy.start()
    below, above = (z + rows - 1) // rows, (2 * rows - 2 - z) // rows
    pl.semaphore_wait(barrier, len(bits) + len(others) + below + above)

    def slot(t, member, q):
        return panel.at[pl.ds(pl.multiple_of(t * tile_rows + member * own + q * piece, piece), piece)]

    def packed(t, place):
        return t - (t - place - 1 + rows) // rows

    def z_copy(t, q, step, first=False, sending=True):
        at = z if sending else z - step
        source = slot(t, p, q)
        if first:
            source = density.at[pl.ds(pl.multiple_of(p * own + q * piece, piece), piece)]
        return pltpu.make_async_remote_copy(
            source, slot(t, p, q), z_send.at[t + (1 - step) // 2, q],
            z_recv.at[packed(t, at + step), q],
            device_id={"row": z + step}, device_id_type=MESH)

    def r_copies(t, q, stage):
        members = [p]
        for bit in bits[:stage]:
            members = members + [flip(member, bit) for member in members]
        peer = flip(p, bits[stage])
        base = 2 ** stage - 1
        return [
            pltpu.make_async_remote_copy(
                slot(t, member, q), slot(t, member, q), r_send.at[base + i, packed(t, z), q],
                r_recv.at[base + i, packed(t, z), q], device_id={"rep": peer}, device_id_type=MESH)
            for i, member in enumerate(members)
        ]

    def r_waits(t, q, stage):
        peer = flip(p, bits[stage])
        members = [peer]
        for bit in bits[:stage]:
            members = members + [flip(member, bit) for member in members]
        base = 2 ** stage - 1
        for i, member in enumerate(members):
            pltpu.make_async_remote_copy(
                slot(t, member, q), slot(t, member, q), r_send.at[base + i, packed(t, z), q],
                r_recv.at[base + i, packed(t, z), q], device_id={"rep": peer}, device_id_type=MESH).wait_recv()

    def a_copy(owner, peer, part):
        return pltpu.make_async_remote_copy(
            density.at[pl.ds(pl.multiple_of(p * own, own), own), pl.ds(part * tile_rows, tile_rows)],
            left.at[owner * ratio + part], a_send.at[peer, part], a_recv.at[owner, part],
            device_id={"col": peer}, device_id_type=MESH)

    def l_copy(owner, peer, part):
        return pltpu.make_async_remote_copy(
            low.at[owner * ratio + part], low.at[owner * ratio + part],
            l_send.at[peer, part], l_recv.at[owner, part],
            device_id={"col": peer}, device_id_type=MESH)

    ways = ((1, z < rows - 1), (-1, z > 0))
    for q in range(chunks):
        for step, ok in ways:
            @pl.when(ok)
            def _():
                z_copy(z, q, step, True).start()
    for other in others:
        for part in range(ratio):
            a_copy(c, other, part).start()

    def arrivals(distance):
        return ((1, z - distance, z - distance >= 0, z < rows - 1),
                (-1, z + distance, z + distance < rows, z > 0))

    def take(distance):
        for q in range(chunks):
            for step, t, ok, onward in arrivals(distance):
                @pl.when(ok)
                def _():
                    z_copy(t, q, step, sending=False).wait_recv()

                    @pl.when(onward)
                    def _():
                        z_copy(t, q, step).start()
                    for copy in r_copies(t, q, 0):
                        copy.start()

    def spread(distance, stage):
        for q in range(chunks):
            for step, t, ok, onward in arrivals(distance):
                @pl.when(ok)
                def _():
                    r_waits(t, q, stage - 1)
                    for copy in r_copies(t, q, stage):
                        copy.start()

    def product(factor, t):
        return jnp.dot(factor[t], panel[pl.ds(pl.multiple_of(t * tile_rows, tile_rows), tile_rows), :],
                       preferred_element_type=jnp.float32)

    def use(distance):
        for step, t, ok, onward in arrivals(distance):
            @pl.when(ok)
            def _():
                for q in range(chunks):
                    r_waits(t, q, len(bits) - 1)
                total[...] += product(left, t)

    keep_tile.wait()
    for copy in keep_left:
        copy.wait()
    started = False
    for distance in range(1, rows + len(bits)):
        if distance < rows:
            take(distance)
        for stage in range(1, len(bits)):
            if 1 <= distance - stage < rows:
                spread(distance - stage, stage)
        if not started:
            for other in others:
                for part in range(ratio):
                    a_copy(other, other, part).wait_recv()
            total[...] = product(left, z)
            started = True
        if 1 <= distance - len(bits) < rows:
            use(distance - len(bits))

    row_block = (p * own + lax.broadcasted_iota(jnp.int32, (own, block), 0)) // block

    def widen(keep, column):
        wide = jnp.zeros((own, block), jnp.float32)
        for i in range(tile_rows // block):
            wide = jnp.where(row_block == i, keep[i, column].astype(jnp.float32), wide)
        return wide

    per_part = tile_rows // block
    for column in range(tile_cols // block):
        span = pl.ds(column * block, block)
        square = total[:, span] * widen(keep_square, column)
        total[:, span] = square
        low[c * ratio + column // per_part, :, pl.ds(column % per_part * block, block)] = square.astype(jnp.bfloat16)
    for other in others:
        for part in range(ratio):
            l_copy(c, other, part).start()
    cube = product(low, c * ratio)
    for part in range(1, ratio):
        cube = cube + product(low, c * ratio + part)
    out[...] = cube
    for other in others:
        for part in range(ratio):
            l_copy(other, other, part).wait_recv()
            out[...] += product(low, other * ratio + part)
    for column in range(tile_cols // block):
        span = pl.ds(column * block, block)
        out[:, span] = 3.0 * total[:, span] - 2.0 * (out[:, span] * widen(keep_cube, column))

    for q in range(chunks):
        for step, ok in ways:
            @pl.when(ok)
            def _():
                z_copy(z, q, step, True).wait_send()
        for distance in range(1, rows):
            for step, t, ok, onward in arrivals(distance):
                @pl.when(ok)
                def _():
                    @pl.when(onward)
                    def _():
                        z_copy(t, q, step).wait_send()
                    for stage in range(len(bits)):
                        for copy in r_copies(t, q, stage):
                            copy.wait_send()
    for other in others:
        for part in range(ratio):
            a_copy(c, other, part).wait_send()
            l_copy(c, other, part).wait_send()


def by_panel(rows, cols, reps, mat, density, keep_square, keep_cube):
    tile_rows, tile_cols = density.shape
    block = tile_rows // keep_square.shape[0]
    own = tile_rows // reps
    ratio = tile_cols // tile_rows
    chunks = 3 if own % 48 == 0 else 1
    dma = pltpu.SemaphoreType.DMA
    return pl.pallas_call(
        functools.partial(panel_kernel, rows, cols, reps, block, chunks),
        out_shape=pltpu.VMEM((own, tile_cols), jnp.float32),
        in_specs=[
            pl.BlockSpec(memory_space=pl.ANY),
            pl.BlockSpec(memory_space=pltpu.SMEM),
            pl.BlockSpec(memory_space=pltpu.SMEM),
        ],
        out_specs=pl.BlockSpec(memory_space=pltpu.VMEM),
        scratch_shapes=[
            pltpu.VMEM((mat, tile_cols), jnp.bfloat16),
            pltpu.VMEM((rows, own, tile_rows), jnp.bfloat16),
            pltpu.VMEM((rows, own, tile_rows), jnp.bfloat16),
            pltpu.VMEM((own, tile_cols), jnp.float32),
            dma((rows + 1, chunks)),
            dma((rows - 1, chunks)),
            dma((reps - 1, rows - 1, chunks)),
            dma((reps - 1, rows - 1, chunks)),
            dma((cols, ratio)),
            dma((cols, ratio)),
            dma((cols, ratio)),
            dma((cols, ratio)),
            dma((1 + ratio,)),
        ],
        compiler_params=pltpu.CompilerParams(collective_id=0, has_side_effects=True),
    )(density, keep_square, keep_cube)


ARRIVALS = {"x_keep": 1, "x_own": 4, "y_own": 3, "z_diag": 1, "z_off": 4, "y_off": 1, "c_part": 4, "x_part": 4,
            "y_part": 4, "v_part": 4, "t_far": 1, "t_diag": 1, "t_off": 1, "t_part": 1}
SENDS = {"x_keep": 0, "x_own": 1, "y_own": 1, "z_diag": 2, "z_off": 2, "y_off": 2, "c_part": 6, "x_part": 3,
         "y_part": 3, "v_part": 3, "t_far": 4, "t_off": 4, "t_diag": 5, "t_part": 5}


def whole_kernel(reps, block, density, keep_square, keep_cube_in, out,
                 tiles, cross, corner, keeps, keep_cube, square, low, keep_wide, local_sem, ready, sends, *sems):
    arrivals = dict(zip(ARRIVALS, sems))
    tile, wide = density.shape
    own = tile // reps
    strips = tile // block
    sub = block // reps
    every = range(strips)
    z, c, p = lax.axis_index("row"), lax.axis_index("col"), lax.axis_index("rep")
    half, here = z // 2, z % 2
    there, other, far = 1 - here, 1 - half, 1 - c
    across = p + reps // 2 - reps * (p // (reps // 2))
    twin = p + 1 - 2 * (p % 2)
    is_diag, is_inner = c == half, here != half
    to_far, to_mate = {"col": far}, {"row": z + 1 - 2 * here}
    to_across, to_twin, to_corner = {"rep": across}, {"rep": twin}, {"col": far, "rep": across}
    quarters = (p, across)
    twins = (twin, across + 1 - 2 * (across % 2))
    distant = (3 * other, other + 1)
    near, end = 1 - other, other
    from_far, from_diag = (0, 2), (1, 3)

    def remote(source, target, name, index, device):
        return pltpu.make_async_remote_copy(
            source, target, sends.at[SENDS[name]], arrivals[name].at[index], device_id=device, device_id_type=MESH)

    def bulk(width):
        blocks = width * sub // block
        many = next(m for m in range(wide // block, 0, -1)
                    if blocks % (16 * m) == 0 and blocks // m <= tile)
        return cross.at[pl.ds(0, blocks // many), pl.ds(0, many * block)]

    def arrived(name, index, width):
        ref = bulk(width)
        remote(ref, ref, name, index, to_mate).wait_recv()

    def sent(name, width):
        ref = bulk(width)
        remote(ref, ref, name, 0, to_mate).wait_send()

    def rows(q, s):
        return pl.ds(pl.multiple_of(s * block + q * sub, sub), sub)

    def columns(start, size):
        return pl.ds(pl.multiple_of(start, block), size)

    def level_at(level):
        return columns(level * tile, tile)

    def relay(ref, name, index, device):
        return remote(ref, ref, name, index, device)

    def own_out(name, j, s, device):
        at = rows(quarters[j], s)
        index = s if j == 0 else strips
        return remote(density.at[at], tiles.at[c, here, at], name, index, device)

    def tile_at(column, level, q, s):
        return tiles.at[column, level, rows(q, s)]

    def diag_at(level, q, s):
        return tiles.at[half, level, rows(q, s), columns(level * tile + s * block, tile - s * block)]

    def part_at(i, q, of=other, source=False):
        if i < strips:
            band = of * i + (1 - of) * (strips - 1 - i)
            ref = (density if i in from_far else tiles.at[half, here]) if source else cross
            return [ref.at[rows(q, band), columns(of * i * block, wide - i * block)]]
        if source:
            return [diag_at(here, q, s) for s in every]
        return [corner.at[rows(q, s), columns(s * block, tile - s * block)] for s in every]

    triangle = sum(tile - s * block for s in every)
    part_width = [wide - s * block for s in every] + [triangle]

    def part_out(i, d):
        for source, target in zip(part_at(i, p, half, True), part_at(i, p, half)):
            remote(source, target, "c_part", i, {"row": distant[d]}).start()

    def part_on(name, i, q, device, index=None):
        for ref in part_at(i, q):
            relay(ref, name, i if index is None else index, device).start()

    def twin_part(j, i):
        part_on("t_part", i, quarters[j], to_twin, 0)

    def twin_tile(name, column, level, j, s):
        relay(tile_at(column, level, quarters[j], s), name, 0, to_twin).start()

    def twin_diag(j):
        for s in every:
            relay(diag_at(there, quarters[j], s), "t_diag", 0, to_twin).start()

    def keep_copy(at):
        return remote(keep_square, keeps.at[at], "x_keep", 0, to_far)

    def spread(i):
        arrived("c_part", i, part_width[i])
        part_on("v_part", i, p, to_corner)
        part_on("y_part", i, p, to_across)
        part_on("x_part", i, p, to_far)
        twin_part(0, i)

    def gather(mine, theirs):
        for i in theirs:
            arrived("x_part", i, part_width[i])
            twin_part(0, i)
        for i in mine:
            arrived("y_part", i, part_width[i])
            twin_part(1, i)
        for i in theirs:
            arrived("v_part", i, part_width[i])
            twin_part(1, i)

    barrier = pltpu.get_barrier_semaphore()
    beside = (to_far, to_mate, to_across, to_twin)
    for device in beside:
        pl.semaphore_signal(barrier, inc=1, device_id=device, device_id_type=MESH)
    is_low = half == 0

    @pl.when(is_low)
    def _():
        for at in distant:
            pl.semaphore_signal(barrier, inc=1, device_id={"row": at}, device_id_type=MESH)

    tile_copy = pltpu.make_async_copy(density, tiles.at[c, here], local_sem.at[0])
    tile_copy.start()
    keep_local = pltpu.make_async_copy(keep_square, keeps.at[c], local_sem.at[1])
    keep_local.start()
    keep_cube_copy = pltpu.make_async_copy(keep_cube_in, keep_cube, local_sem.at[2])
    keep_cube_copy.start()

    row_block = (p * own + lax.broadcasted_iota(jnp.int32, (own, block), 0)) // block

    def widen(at, keep, scale):
        for column in range(wide // block):
            value = jnp.zeros((own, block), jnp.float32)
            for i in range(tile // block):
                value = jnp.where(row_block == i, keep(i, column).astype(jnp.float32) * scale, value)
            keep_wide[at, :, pl.ds(column * block, block)] = value

    def parts_out(parts):
        for d in range(2):
            for i in parts:
                part_out(i, d)

    def granted():
        @pl.when(is_low)
        def _():
            pl.semaphore_wait(ready, 1)

    @pl.when(is_low)
    def _():
        pl.semaphore_wait(barrier, len(beside))

    @pl.when(jnp.logical_not(is_low))
    def _():
        pl.semaphore_wait(barrier, len(beside) + 2)

        @pl.when(is_inner)
        def _():
            for at in distant:
                pl.semaphore_signal(ready, inc=1, device_id={"row": at}, device_id_type=MESH)

        @pl.when(is_diag & is_inner)
        def _():
            parts_out(from_far)

    keep_copy(c).start()
    first = (1, 0) + tuple(range(2, strips))
    for s in first:
        own_out("x_own", 0, s, to_far).start()

    @pl.when(is_diag)
    def _():
        for s in every:
            own_out("x_own", 1, s, to_far).start()
        for j in range(2):
            for s in every:
                remote(density.at[rows(quarters[j], s), columns(here * tile + s * block, tile - s * block)],
                       diag_at(here, quarters[j], s), "z_diag", 0, to_mate).start()

        for s in first:
            arrived("x_own", s, wide)
            if s == first[2]:
                granted()

                @pl.when(is_low & is_inner)
                def _():
                    parts_out(from_far)
            relay(tile_at(other, here, p, s), "y_own", s, to_across).start()
            relay(tile_at(other, here, p, s), "z_off", s, to_mate).start()
            twin_tile("t_far", other, here, 0, s)
        arrived("z_diag", 0, 2 * triangle)
        for j in range(2):
            twin_diag(j)
        @pl.when(jnp.logical_not(is_inner))
        def _():
            spread(1)
        for s in every:
            arrived("y_own", s, wide)
            relay(tile_at(other, here, across, s), "z_off", strips, to_mate).start()
            twin_tile("t_far", other, here, 1, s)
        @pl.when(is_inner)
        def _():
            spread(1)
        spread(strips)
        for s in every:
            arrived("z_off", s, wide)
            twin_tile("t_off", other, there, 0, s)

    @pl.when(jnp.logical_not(is_diag))
    def _():
        for s in every:
            own_out("z_off", 0, s, to_mate).start()
        for s in every:
            arrived("z_off", s, wide)
            relay(tile_at(other, there, p, s), "y_off", 0, to_across).start()
            twin_tile("t_off", other, there, 0, s)

        def pass_far(j, s):
            relay(diag_at(here, quarters[j], s), "z_diag", 0, to_mate).start()
            twin_tile("t_far", half, here, j, s)

        for s in first:
            arrived("x_own", s, wide)
            if s == first[0]:
                granted()

                @pl.when(is_inner)
                def _():
                    parts_out((1,))

            @pl.when(jnp.logical_not(is_inner))
            def _():
                remote(diag_at(here, p, s), part_at(strips, p, half)[s], "c_part", strips,
                       {"row": distant[0]}).start()
            pass_far(0, s)

        @pl.when(jnp.logical_not(is_inner))
        def _():
            part_out(strips, 1)
        for i in from_far:
            spread(i)
        arrived("x_own", strips, strips * wide)
        for s in every:
            pass_far(1, s)
        arrived("y_off", 0, strips * wide)
        for s in every:
            twin_tile("t_off", other, there, 1, s)
        arrived("z_diag", 0, 2 * triangle)
        for j in range(2):
            twin_diag(j)

    tile_copy.wait()
    keep_cube_copy.wait()
    widen(2, lambda i, j: keep_cube[i, j], -2.0)
    keep_local.wait()
    widen(c, lambda i, j: keeps[c, i, j], 1.0)
    keep_copy(far).wait_recv()
    widen(far, lambda i, j: keeps[far, i, j], 1.0)

    def dot(a, b, contract=0):
        return lax.dot_general(a, b, (((1,), (contract,)), ((), ())), preferred_element_type=jnp.float32)

    def complete(ref, lead, level, source_first):
        for a in every:
            for b in range(a + 1, strips):
                r, t = (a, b) if source_first is None else (b + source_first * (a - b), a + source_first * (b - a))
                block_at = lambda i, j: lead + (columns(i * block, block), columns(level * tile + j * block, block))
                ref[block_at(t, r)] = ref[block_at(r, t)].T

    def by_diag(left_here, left_there):
        a = tiles[half, here, :, level_at(here)]
        b = tiles[half, here, :, level_at(there)]
        d = tiles[half, there, :, level_at(there)]
        return dot(left_here, a) + dot(left_there, b, 1), dot(left_here, b) + dot(left_there, d)

    def by_cross(left_near, left_end):
        a = cross[:, level_at(near)]
        b = cross[:, level_at(end)]
        return dot(left_near, a) + dot(left_end, b, 1), dot(left_near, b) + dot(left_end, corner[...])

    my_rows = pl.ds(pl.multiple_of(p * own, own), own)

    arrived("t_diag", 0, 2 * triangle)
    arrived("t_far", 0, 2 * strips * wide)
    complete(tiles, (half, there), there, None)
    lh = [tiles[half, here, my_rows, level_at(level)] for level in (here, there)]
    lo = tiles[other, here, my_rows, :]
    h_here, h_there = by_diag(*lh)
    square[half, :, level_at(here)] = h_here + dot(lo, tiles[other, here], 1)
    square[half, :, level_at(there)] = h_there
    square[other] = dot(lh[0], tiles[other, here])

    @pl.when(is_diag)
    def _():
        arrived("z_off", strips, strips * wide)
        for s in every:
            twin_tile("t_off", other, there, 1, s)
        gather(from_diag, from_far)

    @pl.when(jnp.logical_not(is_diag))
    def _():
        gather(from_far, from_diag)

    arrived("t_off", 0, 2 * strips * wide)

    def mask(at):
        value = square[at] * keep_wide[at]
        square[at] = value
        low[at] = value.astype(jnp.bfloat16)

    square[half, :, level_at(there)] += dot(lo, tiles[other, there], 1)
    mask(half)
    square[other] += dot(lh[1], tiles[other, there])

    @pl.when(is_diag)
    def _():
        h_here, h_there = by_diag(low[half, :, level_at(here)], low[half, :, level_at(there)])
        out[:, level_at(here)] = h_here
        out[:, level_at(there)] = h_there

    @pl.when(jnp.logical_not(is_diag))
    def _():
        out[...] = (dot(low[half, :, level_at(here)], tiles[other, here])
                    + dot(low[half, :, level_at(there)], tiles[other, there]))

    arrived("t_part", 0, 2 * sum(part_width))
    complete(cross, (), near, other)
    complete(corner, (), 0, None)
    o_near, o_end = by_cross(*(tiles[other, here, my_rows, level_at(level)] for level in (near, end)))
    square[other, :, level_at(near)] += o_near
    square[other, :, level_at(end)] += o_end
    mask(other)

    @pl.when(is_diag)
    def _():
        for level in (here, there):
            span = level_at(level)
            cube = out[:, span] + dot(low[other], tiles[other, level], 1)
            out[:, span] = 3.0 * square[c, :, span] + cube * keep_wide[2, :, span]

    @pl.when(jnp.logical_not(is_diag))
    def _():
        cubes = by_cross(low[other, :, level_at(near)], low[other, :, level_at(end)])
        for level, part in zip((near, end), cubes):
            span = level_at(level)
            cube = out[:, span] + part
            out[:, span] = 3.0 * square[c, :, span] + cube * keep_wide[2, :, span]

    keep_copy(c).wait_send()
    sent("t_off", 4 * strips * wide)
    sent("t_part", 2 * triangle + 2 * sum(part_width))

    @pl.when(is_diag)
    def _():
        sent("x_own", 3 * strips * wide)
        sent("z_off", 2 * strips * wide + 2 * triangle)
        sent("x_part", 3 * sum(part_width[i] for i in from_diag))

        @pl.when(is_inner)
        def _():
            sent("c_part", 2 * sum(part_width[i] for i in from_far))

    @pl.when(jnp.logical_not(is_diag))
    def _():
        sent("x_own", strips * wide)
        sent("z_off", 2 * strips * wide + 2 * triangle)
        sent("x_part", 3 * sum(part_width[i] for i in from_far))

        @pl.when(is_inner)
        def _():
            sent("c_part", 2 * part_width[1])

        @pl.when(jnp.logical_not(is_inner))
        def _():
            sent("c_part", 2 * part_width[strips])


def by_whole(reps, density, keep_square, keep_cube):
    tile, wide = density.shape
    block = tile // keep_square.shape[0]
    own = tile // reps
    strips = tile // block
    dma = pltpu.SemaphoreType.DMA
    low = jnp.bfloat16
    return pl.pallas_call(
        functools.partial(whole_kernel, reps, block),
        out_shape=pltpu.VMEM((own, wide), jnp.float32),
        in_specs=[
            pl.BlockSpec(memory_space=pl.ANY),
            pl.BlockSpec(memory_space=pl.ANY),
            pl.BlockSpec(memory_space=pl.ANY),
        ],
        out_specs=pl.BlockSpec(memory_space=pltpu.VMEM),
        scratch_shapes=[
            pltpu.VMEM((2, 2, tile, wide), low),
            pltpu.VMEM((tile, wide), low),
            pltpu.VMEM((tile, tile), low),
            pltpu.SMEM((2,) + keep_square.shape, jnp.int32),
            pltpu.SMEM(keep_cube.shape, jnp.int32),
            pltpu.VMEM((2, own, wide), jnp.float32),
            pltpu.VMEM((2, own, wide), low),
            pltpu.VMEM((3, own, wide), jnp.float32),
            dma((3,)),
            pltpu.SemaphoreType.REGULAR,
            dma((max(SENDS.values()) + 1,)),
        ] + [dma((count,)) for count in ARRIVALS.values()],
        compiler_params=pltpu.CompilerParams(collective_id=0, has_side_effects=True),
    )(density, keep_square, keep_cube)


def solution(mesh):
    rows, cols, reps = (mesh.shape[axis] for axis in ("row", "col", "rep"))

    def body(density, keep_square, keep_cube):
        tile, wide = density.shape
        if cols == 2 and rows == 2 * cols and reps == 4 and tile * rows == wide * cols:
            return by_whole(reps, density, keep_square, keep_cube)
        return by_panel(rows, cols, reps, tile * rows, density, keep_square, keep_cube)

    return jax.shard_map(
        body,
        mesh=mesh,
        in_specs=(P("row", "col"), P("row", "col"), P("row", "col")),
        out_specs=P(("row", "rep"), "col"),
        check_vma=False,
    )
```

```python
import functools

import jax
import jax.numpy as jnp
from jax import lax
from jax.experimental import pallas as pl
from jax.experimental.pallas import tpu as pltpu
from jax.sharding import PartitionSpec as P

MESH = pl.DeviceIdType.MESH

def flip(index, bit):
    return index + bit - 2 * bit * (index // bit % 2)


def panel_kernel(rows, cols, reps, block, chunks, density, keep_square, keep_cube, out,
           panel, left, low, total, z_send, z_recv, r_send, r_recv, a_send, a_recv,
           l_send, l_recv, local_sem):
    tile_rows, tile_cols = density.shape
    own = tile_rows // reps
    piece = own // chunks
    ratio = tile_cols // tile_rows
    z, c, p = lax.axis_index("row"), lax.axis_index("col"), lax.axis_index("rep")
    bits = []
    bit = reps // 2
    while bit:
        bits.append(bit)
        bit //= 2
    others = [lax.rem(c + step, cols) for step in range(1, cols)]

    barrier = pltpu.get_barrier_semaphore()
    for step, ok in ((1, z < rows - 1), (-1, z > 0)):
        @pl.when(ok)
        def _():
            pl.semaphore_signal(barrier, inc=1, device_id={"row": z + step}, device_id_type=MESH)
    for bit in bits:
        pl.semaphore_signal(barrier, inc=1, device_id={"rep": flip(p, bit)}, device_id_type=MESH)
    for other in others:
        pl.semaphore_signal(barrier, inc=1, device_id={"col": other}, device_id_type=MESH)
    keep_tile = pltpu.make_async_copy(
        density, panel.at[pl.ds(pl.multiple_of(z * tile_rows, tile_rows), tile_rows)], local_sem.at[0])
    keep_tile.start()
    keep_left = [
        pltpu.make_async_copy(
            density.at[pl.ds(pl.multiple_of(p * own, own), own), pl.ds(part * tile_rows, tile_rows)],
            left.at[c * ratio + part], local_sem.at[1 + part])
        for part in range(ratio)
    ]
    for copy in keep_left:
        copy.start()
    below, above = (z + rows - 1) // rows, (2 * rows - 2 - z) // rows
    pl.semaphore_wait(barrier, len(bits) + len(others) + below + above)

    def slot(t, member, q):
        return panel.at[pl.ds(pl.multiple_of(t * tile_rows + member * own + q * piece, piece), piece)]

    def packed(t, place):
        return t - (t - place - 1 + rows) // rows

    def z_copy(t, q, step, first=False, sending=True):
        at = z if sending else z - step
        source = slot(t, p, q)
        if first:
            source = density.at[pl.ds(pl.multiple_of(p * own + q * piece, piece), piece)]
        return pltpu.make_async_remote_copy(
            source, slot(t, p, q), z_send.at[t + (1 - step) // 2, q],
            z_recv.at[packed(t, at + step), q],
            device_id={"row": z + step}, device_id_type=MESH)

    def r_copies(t, q, stage):
        members = [p]
        for bit in bits[:stage]:
            members = members + [flip(member, bit) for member in members]
        peer = flip(p, bits[stage])
        base = 2 ** stage - 1
        return [
            pltpu.make_async_remote_copy(
                slot(t, member, q), slot(t, member, q), r_send.at[base + i, packed(t, z), q],
                r_recv.at[base + i, packed(t, z), q], device_id={"rep": peer}, device_id_type=MESH)
            for i, member in enumerate(members)
        ]

    def r_waits(t, q, stage):
        peer = flip(p, bits[stage])
        members = [peer]
        for bit in bits[:stage]:
            members = members + [flip(member, bit) for member in members]
        base = 2 ** stage - 1
        for i, member in enumerate(members):
            pltpu.make_async_remote_copy(
                slot(t, member, q), slot(t, member, q), r_send.at[base + i, packed(t, z), q],
                r_recv.at[base + i, packed(t, z), q], device_id={"rep": peer}, device_id_type=MESH).wait_recv()

    def a_copy(owner, peer, part):
        return pltpu.make_async_remote_copy(
            density.at[pl.ds(pl.multiple_of(p * own, own), own), pl.ds(part * tile_rows, tile_rows)],
            left.at[owner * ratio + part], a_send.at[peer, part], a_recv.at[owner, part],
            device_id={"col": peer}, device_id_type=MESH)

    def l_copy(owner, peer, part):
        return pltpu.make_async_remote_copy(
            low.at[owner * ratio + part], low.at[owner * ratio + part],
            l_send.at[peer, part], l_recv.at[owner, part],
            device_id={"col": peer}, device_id_type=MESH)

    ways = ((1, z < rows - 1), (-1, z > 0))
    for q in range(chunks):
        for step, ok in ways:
            @pl.when(ok)
            def _():
                z_copy(z, q, step, True).start()
    for other in others:
        for part in range(ratio):
            a_copy(c, other, part).start()

    def arrivals(distance):
        return ((1, z - distance, z - distance >= 0, z < rows - 1),
                (-1, z + distance, z + distance < rows, z > 0))

    def take(distance):
        for q in range(chunks):
            for step, t, ok, onward in arrivals(distance):
                @pl.when(ok)
                def _():
                    z_copy(t, q, step, sending=False).wait_recv()

                    @pl.when(onward)
                    def _():
                        z_copy(t, q, step).start()
                    for copy in r_copies(t, q, 0):
                        copy.start()

    def spread(distance, stage):
        for q in range(chunks):
            for step, t, ok, onward in arrivals(distance):
                @pl.when(ok)
                def _():
                    r_waits(t, q, stage - 1)
                    for copy in r_copies(t, q, stage):
                        copy.start()

    def product(factor, t):
        return jnp.dot(factor[t], panel[pl.ds(pl.multiple_of(t * tile_rows, tile_rows), tile_rows), :],
                       preferred_element_type=jnp.float32)

    def use(distance):
        for step, t, ok, onward in arrivals(distance):
            @pl.when(ok)
            def _():
                for q in range(chunks):
                    r_waits(t, q, len(bits) - 1)
                total[...] += product(left, t)

    keep_tile.wait()
    for copy in keep_left:
        copy.wait()
    started = False
    for distance in range(1, rows + len(bits)):
        if distance < rows:
            take(distance)
        for stage in range(1, len(bits)):
            if 1 <= distance - stage < rows:
                spread(distance - stage, stage)
        if not started:
            for other in others:
                for part in range(ratio):
                    a_copy(other, other, part).wait_recv()
            total[...] = product(left, z)
            started = True
        if 1 <= distance - len(bits) < rows:
            use(distance - len(bits))

    row_block = (p * own + lax.broadcasted_iota(jnp.int32, (own, block), 0)) // block

    def widen(keep, column):
        wide = jnp.zeros((own, block), jnp.float32)
        for i in range(tile_rows // block):
            wide = jnp.where(row_block == i, keep[i, column].astype(jnp.float32), wide)
        return wide

    per_part = tile_rows // block
    for column in range(tile_cols // block):
        span = pl.ds(column * block, block)
        square = total[:, span] * widen(keep_square, column)
        total[:, span] = square
        low[c * ratio + column // per_part, :, pl.ds(column % per_part * block, block)] = square.astype(jnp.bfloat16)
    for other in others:
        for part in range(ratio):
            l_copy(c, other, part).start()
    cube = product(low, c * ratio)
    for part in range(1, ratio):
        cube = cube + product(low, c * ratio + part)
    out[...] = cube
    for other in others:
        for part in range(ratio):
            l_copy(other, other, part).wait_recv()
            out[...] += product(low, other * ratio + part)
    for column in range(tile_cols // block):
        span = pl.ds(column * block, block)
        out[:, span] = 3.0 * total[:, span] - 2.0 * (out[:, span] * widen(keep_cube, column))

    for q in range(chunks):
        for step, ok in ways:
            @pl.when(ok)
            def _():
                z_copy(z, q, step, True).wait_send()
        for distance in range(1, rows):
            for step, t, ok, onward in arrivals(distance):
                @pl.when(ok)
                def _():
                    @pl.when(onward)
                    def _():
                        z_copy(t, q, step).wait_send()
                    for stage in range(len(bits)):
                        for copy in r_copies(t, q, stage):
                            copy.wait_send()
    for other in others:
        for part in range(ratio):
            a_copy(c, other, part).wait_send()
            l_copy(c, other, part).wait_send()


def by_panel(rows, cols, reps, mat, density, keep_square, keep_cube):
    tile_rows, tile_cols = density.shape
    block = tile_rows // keep_square.shape[0]
    own = tile_rows // reps
    ratio = tile_cols // tile_rows
    chunks = 3 if own % 48 == 0 else 1
    dma = pltpu.SemaphoreType.DMA
    return pl.pallas_call(
        functools.partial(panel_kernel, rows, cols, reps, block, chunks),
        out_shape=pltpu.VMEM((own, tile_cols), jnp.float32),
        in_specs=[
            pl.BlockSpec(memory_space=pl.ANY),
            pl.BlockSpec(memory_space=pltpu.SMEM),
            pl.BlockSpec(memory_space=pltpu.SMEM),
        ],
        out_specs=pl.BlockSpec(memory_space=pltpu.VMEM),
        scratch_shapes=[
            pltpu.VMEM((mat, tile_cols), jnp.bfloat16),
            pltpu.VMEM((rows, own, tile_rows), jnp.bfloat16),
            pltpu.VMEM((rows, own, tile_rows), jnp.bfloat16),
            pltpu.VMEM((own, tile_cols), jnp.float32),
            dma((rows + 1, chunks)),
            dma((rows - 1, chunks)),
            dma((reps - 1, rows - 1, chunks)),
            dma((reps - 1, rows - 1, chunks)),
            dma((cols, ratio)),
            dma((cols, ratio)),
            dma((cols, ratio)),
            dma((cols, ratio)),
            dma((1 + ratio,)),
        ],
        compiler_params=pltpu.CompilerParams(collective_id=0, has_side_effects=True),
    )(density, keep_square, keep_cube)


ARRIVALS = {"x_keep": 1, "x_own": 4, "y_own": 3, "z_diag": 1, "z_off": 4, "y_off": 1, "c_part": 2, "x_part": 2,
            "y_part": 2, "v_part": 2, "t_far": 1, "t_diag": 1, "t_off": 1, "t_part": 1}
SENDS = {"x_keep": 0, "x_own": 1, "y_own": 1, "z_diag": 2, "z_off": 2, "y_off": 2, "c_part": 6, "x_part": 3,
         "y_part": 3, "v_part": 3, "t_far": 4, "t_off": 4, "t_diag": 5, "t_part": 5}


def whole_kernel(reps, block, density, keep_square, keep_cube_in, out,
                 tiles, cross, corner, keeps, keep_cube, square, low, keep_wide, local_sem, ready, sends, *sems):
    arrivals = dict(zip(ARRIVALS, sems))
    tile, wide = density.shape
    own = tile // reps
    strips = tile // block
    sub = block // reps
    every = range(strips)
    z, c, p = lax.axis_index("row"), lax.axis_index("col"), lax.axis_index("rep")
    half, here = z // 2, z % 2
    there, other, far = 1 - here, 1 - half, 1 - c
    across = p + reps // 2 - reps * (p // (reps // 2))
    twin = p + 1 - 2 * (p % 2)
    is_diag, is_inner = c == half, here != half
    to_far, to_mate = {"col": far}, {"row": z + 1 - 2 * here}
    to_across, to_twin, to_corner = {"rep": across}, {"rep": twin}, {"col": far, "rep": across}
    quarters = (p, across)
    twins = (twin, across + 1 - 2 * (across % 2))
    distant = (3 * other, other + 1)
    near, end = 1 - other, other
    from_far, from_diag = (0, 2), (1, 3)

    def remote(source, target, name, index, device):
        return pltpu.make_async_remote_copy(
            source, target, sends.at[SENDS[name]], arrivals[name].at[index], device_id=device, device_id_type=MESH)

    def bulk(width):
        blocks = width * sub // block
        many = next(m for m in range(wide // block, 0, -1)
                    if blocks % (16 * m) == 0 and blocks // m <= tile)
        return cross.at[pl.ds(0, blocks // many), pl.ds(0, many * block)]

    def arrived(name, index, width):
        ref = bulk(width)
        remote(ref, ref, name, index, to_mate).wait_recv()

    def sent(name, width):
        ref = bulk(width)
        remote(ref, ref, name, 0, to_mate).wait_send()

    def rows(q, s):
        return pl.ds(pl.multiple_of(s * block + q * sub, sub), sub)

    def columns(start, size):
        return pl.ds(pl.multiple_of(start, block), size)

    def level_at(level):
        return columns(level * tile, tile)

    def relay(ref, name, index, device):
        return remote(ref, ref, name, index, device)

    def own_out(name, j, s, device):
        at = rows(quarters[j], s)
        index = s if j == 0 else strips
        return remote(density.at[at], tiles.at[c, here, at], name, index, device)

    def tile_at(column, level, q, s):
        return tiles.at[column, level, rows(q, s)]

    def diag_at(level, q, s):
        return tiles.at[half, level, rows(q, s), columns(level * tile + s * block, tile - s * block)]

    def part_at(i, q, of=other, source=False):
        if i < strips:
            band = of * i + (1 - of) * (strips - 1 - i)
            ref = (density if i in from_far else tiles.at[half, here]) if source else cross
            return [ref.at[rows(q, band), columns(of * i * block, wide - i * block)]]
        if source:
            return [diag_at(here, q, s) for s in every]
        return [corner.at[rows(q, s), columns(s * block, tile - s * block)] for s in every]

    triangle = sum(tile - s * block for s in every)
    part_width = [wide - s * block for s in every] + [triangle]

    def part_out(i, d):
        for source, target in zip(part_at(i, p, half, True), part_at(i, p, half)):
            remote(source, target, "c_part", i // 2, {"row": distant[d]}).start()

    def part_on(name, i, q, device, index=None):
        for ref in part_at(i, q):
            relay(ref, name, i // 2 if index is None else index, device).start()

    def twin_part(j, i):
        part_on("t_part", i, quarters[j], to_twin, 0)

    def twin_tile(name, column, level, j, s):
        relay(tile_at(column, level, quarters[j], s), name, 0, to_twin).start()

    def twin_diag(j):
        for s in every:
            relay(diag_at(there, quarters[j], s), "t_diag", 0, to_twin).start()

    def keep_copy(at):
        return remote(keep_square, keeps.at[at], "x_keep", 0, to_far)

    def spread(i):
        arrived("c_part", i // 2, part_width[i])
        part_on("v_part", i, p, to_corner)
        part_on("y_part", i, p, to_across)
        part_on("x_part", i, p, to_far)
        twin_part(0, i)

    def gather(mine, theirs):
        for i in theirs:
            arrived("x_part", i // 2, part_width[i])
            twin_part(0, i)
        for i in mine:
            arrived("y_part", i // 2, part_width[i])
            twin_part(1, i)
        for i in theirs:
            arrived("v_part", i // 2, part_width[i])
            twin_part(1, i)

    barrier = pltpu.get_barrier_semaphore()
    beside = (to_far, to_mate, to_across, to_twin)
    for device in beside:
        pl.semaphore_signal(barrier, inc=1, device_id=device, device_id_type=MESH)
    is_low = half == 0

    @pl.when(is_low)
    def _():
        for at in distant:
            pl.semaphore_signal(barrier, inc=1, device_id={"row": at}, device_id_type=MESH)

    tile_copy = pltpu.make_async_copy(density, tiles.at[c, here], local_sem.at[0])
    tile_copy.start()
    keep_local = pltpu.make_async_copy(keep_square, keeps.at[c], local_sem.at[1])
    keep_local.start()
    keep_cube_copy = pltpu.make_async_copy(keep_cube_in, keep_cube, local_sem.at[2])
    keep_cube_copy.start()

    row_block = (p * own + lax.broadcasted_iota(jnp.int32, (own, block), 0)) // block

    def widen(at, keep, scale):
        for column in range(wide // block):
            value = jnp.zeros((own, block), jnp.float32)
            for i in range(tile // block):
                value = jnp.where(row_block == i, keep(i, column).astype(jnp.float32) * scale, value)
            keep_wide[at, :, pl.ds(column * block, block)] = value

    def parts_out(parts):
        for d in range(2):
            for i in parts:
                part_out(i, d)

    def granted():
        @pl.when(is_low)
        def _():
            pl.semaphore_wait(ready, 1)

    @pl.when(is_low)
    def _():
        pl.semaphore_wait(barrier, len(beside))

    @pl.when(jnp.logical_not(is_low))
    def _():
        pl.semaphore_wait(barrier, len(beside) + 2)

        @pl.when(is_inner)
        def _():
            for at in distant:
                pl.semaphore_signal(ready, inc=1, device_id={"row": at}, device_id_type=MESH)

        @pl.when(is_diag & is_inner)
        def _():
            parts_out(from_far)

    keep_copy(c).start()
    first = (1, 0) + tuple(range(2, strips))
    for s in first:
        own_out("x_own", 0, s, to_far).start()

    @pl.when(is_diag)
    def _():
        for s in every:
            own_out("x_own", 1, s, to_far).start()
        for j in range(2):
            for s in every:
                remote(density.at[rows(quarters[j], s), columns(here * tile + s * block, tile - s * block)],
                       diag_at(here, quarters[j], s), "z_diag", 0, to_mate).start()

        for s in first:
            arrived("x_own", s, wide)
            if s == first[2]:
                granted()

                @pl.when(is_low & is_inner)
                def _():
                    parts_out(from_far)
            relay(tile_at(other, here, p, s), "y_own", s, to_across).start()
            relay(tile_at(other, here, p, s), "z_off", s, to_mate).start()
            twin_tile("t_far", other, here, 0, s)
        arrived("z_diag", 0, 2 * triangle)
        for j in range(2):
            twin_diag(j)
        @pl.when(jnp.logical_not(is_inner))
        def _():
            spread(1)
        for s in every:
            arrived("y_own", s, wide)
            relay(tile_at(other, here, across, s), "z_off", strips, to_mate).start()
            twin_tile("t_far", other, here, 1, s)
        @pl.when(is_inner)
        def _():
            spread(1)
        spread(strips)
        for s in every:
            arrived("z_off", s, wide)
            twin_tile("t_off", other, there, 0, s)

    @pl.when(jnp.logical_not(is_diag))
    def _():
        for s in every:
            own_out("z_off", 0, s, to_mate).start()
        for s in every:
            arrived("z_off", s, wide)
            relay(tile_at(other, there, p, s), "y_off", 0, to_across).start()
            twin_tile("t_off", other, there, 0, s)

        def pass_far(j, s):
            relay(diag_at(here, quarters[j], s), "z_diag", 0, to_mate).start()
            twin_tile("t_far", half, here, j, s)

        for s in first:
            arrived("x_own", s, wide)
            if s == first[0]:
                granted()

                @pl.when(is_inner)
                def _():
                    parts_out((1,))

            @pl.when(jnp.logical_not(is_inner))
            def _():
                remote(diag_at(here, p, s), part_at(strips, p, half)[s], "c_part", strips // 2,
                       {"row": distant[0]}).start()
            pass_far(0, s)

        @pl.when(jnp.logical_not(is_inner))
        def _():
            part_out(strips, 1)
        for i in from_far:
            spread(i)
        arrived("x_own", strips, strips * wide)
        for s in every:
            pass_far(1, s)
        arrived("y_off", 0, strips * wide)
        for s in every:
            twin_tile("t_off", other, there, 1, s)
        arrived("z_diag", 0, 2 * triangle)
        for j in range(2):
            twin_diag(j)

    tile_copy.wait()
    keep_cube_copy.wait()
    widen(2, lambda i, j: keep_cube[i, j], -2.0)
    keep_local.wait()
    widen(c, lambda i, j: keeps[c, i, j], 1.0)
    keep_copy(far).wait_recv()
    widen(far, lambda i, j: keeps[far, i, j], 1.0)

    def dot(a, b, contract=0):
        return lax.dot_general(a, b, (((1,), (contract,)), ((), ())), preferred_element_type=jnp.float32)

    def complete(ref, lead, level, source_first):
        for a in every:
            for b in range(a + 1, strips):
                r, t = (a, b) if source_first is None else (b + source_first * (a - b), a + source_first * (b - a))
                block_at = lambda i, j: lead + (columns(i * block, block), columns(level * tile + j * block, block))
                ref[block_at(t, r)] = ref[block_at(r, t)].T

    def by_diag(left_here, left_there):
        a = tiles[half, here, :, level_at(here)]
        b = tiles[half, here, :, level_at(there)]
        d = tiles[half, there, :, level_at(there)]
        return dot(left_here, a) + dot(left_there, b, 1), dot(left_here, b) + dot(left_there, d)

    def by_cross(left_near, left_end):
        a = cross[:, level_at(near)]
        b = cross[:, level_at(end)]
        return dot(left_near, a) + dot(left_end, b, 1), dot(left_near, b) + dot(left_end, corner[...])

    my_rows = pl.ds(pl.multiple_of(p * own, own), own)

    arrived("t_diag", 0, 2 * triangle)
    arrived("t_far", 0, 2 * strips * wide)
    complete(tiles, (half, there), there, None)
    lh = [tiles[half, here, my_rows, level_at(level)] for level in (here, there)]
    lo = tiles[other, here, my_rows, :]
    h_here, h_there = by_diag(*lh)
    square[half, :, level_at(here)] = h_here + dot(lo, tiles[other, here], 1)
    square[half, :, level_at(there)] = h_there
    square[other] = dot(lh[0], tiles[other, here])

    @pl.when(is_diag)
    def _():
        arrived("z_off", strips, strips * wide)
        for s in every:
            twin_tile("t_off", other, there, 1, s)
        gather(from_diag, from_far)

    @pl.when(jnp.logical_not(is_diag))
    def _():
        gather(from_far, from_diag)

    arrived("t_off", 0, 2 * strips * wide)

    def mask(at):
        value = square[at] * keep_wide[at]
        square[at] = value
        low[at] = value.astype(jnp.bfloat16)

    square[half, :, level_at(there)] += dot(lo, tiles[other, there], 1)
    mask(half)
    square[other] += dot(lh[1], tiles[other, there])

    @pl.when(is_diag)
    def _():
        h_here, h_there = by_diag(low[half, :, level_at(here)], low[half, :, level_at(there)])
        out[:, level_at(here)] = h_here
        out[:, level_at(there)] = h_there

    @pl.when(jnp.logical_not(is_diag))
    def _():
        out[...] = (dot(low[half, :, level_at(here)], tiles[other, here])
                    + dot(low[half, :, level_at(there)], tiles[other, there]))

    arrived("t_part", 0, 2 * sum(part_width))
    complete(cross, (), near, other)
    complete(corner, (), 0, None)
    o_near, o_end = by_cross(*(tiles[other, here, my_rows, level_at(level)] for level in (near, end)))
    square[other, :, level_at(near)] += o_near
    square[other, :, level_at(end)] += o_end
    mask(other)

    @pl.when(is_diag)
    def _():
        for level in (here, there):
            span = level_at(level)
            cube = out[:, span] + dot(low[other], tiles[other, level], 1)
            out[:, span] = 3.0 * square[c, :, span] + cube * keep_wide[2, :, span]

    @pl.when(jnp.logical_not(is_diag))
    def _():
        cubes = by_cross(low[other, :, level_at(near)], low[other, :, level_at(end)])
        for level, part in zip((near, end), cubes):
            span = level_at(level)
            cube = out[:, span] + part
            out[:, span] = 3.0 * square[c, :, span] + cube * keep_wide[2, :, span]

    keep_copy(c).wait_send()
    sent("t_off", 4 * strips * wide)
    sent("t_part", 2 * triangle + 2 * sum(part_width))

    @pl.when(is_diag)
    def _():
        sent("x_own", 3 * strips * wide)
        sent("z_off", 2 * strips * wide + 2 * triangle)
        sent("x_part", 3 * sum(part_width[i] for i in from_diag))

        @pl.when(is_inner)
        def _():
            sent("c_part", 2 * sum(part_width[i] for i in from_far))

    @pl.when(jnp.logical_not(is_diag))
    def _():
        sent("x_own", strips * wide)
        sent("z_off", 2 * strips * wide + 2 * triangle)
        sent("x_part", 3 * sum(part_width[i] for i in from_far))

        @pl.when(is_inner)
        def _():
            sent("c_part", 2 * part_width[1])

        @pl.when(jnp.logical_not(is_inner))
        def _():
            sent("c_part", 2 * part_width[strips])


def by_whole(reps, density, keep_square, keep_cube):
    tile, wide = density.shape
    block = tile // keep_square.shape[0]
    own = tile // reps
    strips = tile // block
    dma = pltpu.SemaphoreType.DMA
    low = jnp.bfloat16
    return pl.pallas_call(
        functools.partial(whole_kernel, reps, block),
        out_shape=pltpu.VMEM((own, wide), jnp.float32),
        in_specs=[
            pl.BlockSpec(memory_space=pl.ANY),
            pl.BlockSpec(memory_space=pl.ANY),
            pl.BlockSpec(memory_space=pl.ANY),
        ],
        out_specs=pl.BlockSpec(memory_space=pltpu.VMEM),
        scratch_shapes=[
            pltpu.VMEM((2, 2, tile, wide), low),
            pltpu.VMEM((tile, wide), low),
            pltpu.VMEM((tile, tile), low),
            pltpu.SMEM((2,) + keep_square.shape, jnp.int32),
            pltpu.SMEM(keep_cube.shape, jnp.int32),
            pltpu.VMEM((2, own, wide), jnp.float32),
            pltpu.VMEM((2, own, wide), low),
            pltpu.VMEM((3, own, wide), jnp.float32),
            dma((3,)),
            pltpu.SemaphoreType.REGULAR,
            dma((max(SENDS.values()) + 1,)),
        ] + [dma((count,)) for count in ARRIVALS.values()],
        compiler_params=pltpu.CompilerParams(collective_id=0, has_side_effects=True),
    )(density, keep_square, keep_cube)


def solution(mesh):
    rows, cols, reps = (mesh.shape[axis] for axis in ("row", "col", "rep"))

    def body(density, keep_square, keep_cube):
        tile, wide = density.shape
        if cols == 2 and rows == 2 * cols and reps == 4 and tile * rows == wide * cols:
            return by_whole(reps, density, keep_square, keep_cube)
        return by_panel(rows, cols, reps, tile * rows, density, keep_square, keep_cube)

    return jax.shard_map(
        body,
        mesh=mesh,
        in_specs=(P("row", "col"), P("row", "col"), P("row", "col")),
        out_specs=P(("row", "rep"), "col"),
        check_vma=False,
    )
```
